32 devices in a mesh: gx: 4 (over z), gy: 8 (over y, x, core).
Axes of the slice: x: 2, y: 2, z: 4, core: 2. Of those that a mesh axis runs over, the one named last changes fastest.
Arguments:
- grid_state: bfloat16 [8192, 1024], P(('gx', 'gy')), may hold values from -6 to 6
- mesh_state: bfloat16 [8192, 1024], P(('gx', 'gy')), may hold values from -6 to 6
- encode_block: int32 [8192], P(('gx', 'gy')), may hold values from 0 to 63, as said below
- neighbour_block: int32 [64], P(('gx', 'gy')), may hold values from 0 to 63, as said below
- decode_block: int32 [8192], P(('gx', 'gy')), may hold values from 0 to 63, as said below
- encode_grid_gain: float32 [1024], replicated, may hold values from 0.25 to 1.75
- encode_mesh_gain: float32 [1024], replicated, may hold values from 0.25 to 1.75
- process_gain: float32 [1024], replicated, may hold values from 0.25 to 1.75
- decode_grid_gain: float32 [1024], replicated, may hold values from 0.25 to 1.75
- decode_mesh_gain: float32 [1024], replicated, may hold values from 0.25 to 1.75
- encode_query: bfloat16 [1024, 1024], replicated, may hold values from -0.1875 to 0.1875
- encode_keyval: bfloat16 [1024, 2048], replicated, may hold values from -0.1875 to 0.1875
- encode_out: bfloat16 [1024, 1024], replicated, may hold values from -0.1875 to 0.1875
- process_qkv: bfloat16 [1024, 3072], replicated, may hold values from -0.1875 to 0.1875
- process_out: bfloat16 [1024, 1024], replicated, may hold values from -0.1875 to 0.1875
- decode_query: bfloat16 [1024, 1024], replicated, may hold values from -0.1875 to 0.1875
- decode_keyval: bfloat16 [1024, 2048], replicated, may hold values from -0.1875 to 0.1875
- decode_out: bfloat16 [1024, 1024], replicated, may hold values from -0.1875 to 0.1875
Outputs:
- grid_update: bfloat16 [8192, 1024], P(('gx', 'gy'))
The draws below stay inside these ranges and needn't reach their ends.
Inputs may be any that keep to these rules, and one draw needn't show every extreme that they name: `encode_block`: block b lies on the b // 2-th device of the order of mesh nodes. The grid points of one device name the blocks of one device at most 16 times in all; every block is named by some grid point; in every draw some device's blocks are named exactly 16 times by the grid points of every device. `neighbour_block`: never b itself, and at most two blocks away from b. `decode_block`: block b lies on the b // 2-th device. The grid points of one device name the blocks of one device at most 16 times in all; every block is named; in every draw some device's blocks are named exactly 16 times by the grid points of every device.
All inputs are finite; a program needn't handle non-finite values.
Results may differ from the reference program's by a relative error of at most 0.015.
Values may be sent and summed in bfloat16 or wider, within the bound.
No kernel may reach another device: no remote copies, remote signals or barrier semaphores. Data moves between devices by JAX's collectives and lax.ppermute only.
A program may use at most 128 MiB of HBM per device.

```python
import jax
import jax.numpy as jnp
from jax import lax

D = 1024
HEADS = 16
BLOCK = 128
GRID_DEV = 256
MESH_DEV = 256
CAP = 16
GRID = 8192
MESH = 8192
N_GX = 4
N_GY = 8


def routed_blocks(key):
    devices = N_GX * N_GY
    per_device = MESH_DEV // BLOCK
    total_slots = devices * CAP
    hottest = jax.random.randint(jax.random.fold_in(key, 1), (), 0, devices)
    slot_owner = jnp.arange(total_slots, dtype=jnp.int32) // CAP
    slot_rank = jnp.arange(total_slots, dtype=jnp.int32) % CAP

    def one_source(source):
        subkeys = jax.random.split(jax.random.fold_in(key, source + 7), 3)
        scores = jax.random.permutation(subkeys[0], total_slots).astype(jnp.int32)
        forced = (slot_owner == hottest) | (slot_owner == source) & (slot_rank < per_device)
        scores = scores + forced.astype(jnp.int32) * (2 * total_slots)
        chosen = lax.top_k(scores, GRID_DEV)[1]
        owners = chosen // CAP
        ranks = chosen % CAP
        pinned = (owners == source) & (ranks < per_device)
        spares = jax.random.randint(subkeys[1], (GRID_DEV,), 0, per_device)
        blocks = owners * per_device + jnp.where(pinned, ranks, spares)
        return blocks[jax.random.permutation(subkeys[2], GRID_DEV)]
    return jax.vmap(one_source)(jnp.arange(devices, dtype=jnp.int32)).reshape(-1).astype(jnp.int32)


def draw_encode_block(key, part):
    return routed_blocks(jax.random.fold_in(key, 11))


def draw_decode_block(key, part):
    return routed_blocks(jax.random.fold_in(key, 23))


def draw_neighbour_block(key, part):
    total_blocks = N_GX * N_GY * (MESH_DEV // BLOCK)
    blocks = jnp.arange(total_blocks, dtype=jnp.int32)
    picks = jax.random.randint(jax.random.fold_in(key, 37), (total_blocks,), 0, 4)
    offsets = jnp.where(picks < 2, picks - 2, picks - 1)
    target = blocks + offsets
    outside = (target < 0) | (target >= total_blocks)
    return jnp.where(outside, blocks - offsets, target).astype(jnp.int32)


def levels(own_key, extent, cuts, smallest, largest):
    level, own = 1.0, jax.random.fold_in(own_key, 6)
    for dim, parts in cuts:
        draws = jnp.exp(jax.random.uniform(jax.random.fold_in(own, dim), (parts,), jnp.float32, smallest / len(cuts), largest / len(cuts)))
        level = level * jnp.repeat(draws, extent[dim] // parts).reshape([-1 if axis == dim else 1 for axis in range(len(extent))])
    return level


def bell_draw(own_key, dims, width, limit, cuts=(), kind=jnp.bfloat16):
    factor_of = levels(own_key, dims, cuts, -0.22, 0.18) if cuts else 1.0
    values = jax.random.normal(own_key, dims, jnp.float32) * width * factor_of
    return jnp.minimum(jnp.maximum(values, -limit), limit).astype(kind)


def setup_inputs(seed: int = 0) -> dict:
    key_list = jax.random.split(jax.random.key(seed), 19)
    return {
        "grid_state": bell_draw(key_list[0], (GRID, D), 1.0, 6.0, ((0, 32),)),
        "mesh_state": bell_draw(key_list[1], (MESH, D), 1.0, 6.0, ((0, 32),)),
        "encode_block": draw_encode_block(jax.random.fold_in(key_list[18], 71), 0),
        "neighbour_block": draw_neighbour_block(jax.random.fold_in(key_list[18], 71), 0),
        "decode_block": draw_decode_block(jax.random.fold_in(key_list[18], 71), 0),
        "encode_grid_gain": jnp.clip(1.0 + 0.15 * jax.random.normal(key_list[5], (D,), jnp.float32), 0.25, 1.75),
        "encode_mesh_gain": jnp.clip(1.0 + 0.15 * jax.random.normal(key_list[6], (D,), jnp.float32), 0.25, 1.75),
        "process_gain": jnp.clip(1.0 + 0.15 * jax.random.normal(key_list[7], (D,), jnp.float32), 0.25, 1.75),
        "decode_grid_gain": jnp.clip(1.0 + 0.15 * jax.random.normal(key_list[8], (D,), jnp.float32), 0.25, 1.75),
        "decode_mesh_gain": jnp.clip(1.0 + 0.15 * jax.random.normal(key_list[9], (D,), jnp.float32), 0.25, 1.75),
        "encode_query": bell_draw(key_list[10], (D, D), D ** -0.5, 0.1875),
        "encode_keyval": bell_draw(key_list[11], (D, 2 * D), D ** -0.5, 0.1875),
        "encode_out": bell_draw(key_list[12], (D, D), D ** -0.5, 0.1875),
        "process_qkv": bell_draw(key_list[13], (D, 3 * D), D ** -0.5, 0.1875),
        "process_out": bell_draw(key_list[14], (D, D), D ** -0.5, 0.1875),
        "decode_query": bell_draw(key_list[15], (D, D), D ** -0.5, 0.1875),
        "decode_keyval": bell_draw(key_list[16], (D, 2 * D), D ** -0.5, 0.1875),
        "decode_out": bell_draw(key_list[17], (D, D), D ** -0.5, 0.1875),
    }


masked_score = -1e+30

def norm_rows(values, row_gain):
    wide = values.astype(jnp.float32)
    return wide * lax.rsqrt(lax.optimization_barrier(jnp.mean(wide * wide, axis=-1, keepdims=True)) + 1e-06) * row_gain

def attend(queries, keyval, allowed):
    features = queries.shape[-1]
    head_size = features // HEADS
    query_heads = queries.astype(jnp.float32).reshape(queries.shape[0], HEADS, head_size)
    key_heads = keyval[:, :features].astype(jnp.float32).reshape(keyval.shape[0], HEADS, head_size)
    value_heads = keyval[:, features:].astype(jnp.float32).reshape(keyval.shape[0], HEADS, head_size)
    scores = jnp.einsum('qhd,khd->hqk', query_heads, key_heads) * head_size ** (-0.5)
    scores = jnp.where(allowed[None], scores, masked_score)
    highest = lax.optimization_barrier(jnp.max(scores, axis=-1, keepdims=True))
    powers = jnp.exp(scores - highest)
    chances = (powers / lax.optimization_barrier(jnp.sum(powers, axis=-1, keepdims=True))).astype(jnp.bfloat16)
    output = jnp.einsum('hqk,khd->qhd', chances.astype(jnp.float32), value_heads)
    return output.reshape(queries.shape[0], features).astype(jnp.bfloat16)

def project(values, weight):
    return jnp.dot(values, weight, preferred_element_type=jnp.float32).astype(jnp.bfloat16)

def reference(grid_state, mesh_state, encode_block, neighbour_block, decode_block, encode_grid_gain, encode_mesh_gain, process_gain, decode_grid_gain, decode_mesh_gain, encode_query, encode_keyval, encode_out, process_qkv, process_out, decode_query, decode_keyval, decode_out):
    devices = N_GX * N_GY
    block_count = MESH_DEV // BLOCK
    slot_total = CAP * devices
    grid_count = grid_state.shape[0]
    features = grid_state.shape[1]
    blocks_all = mesh_state.shape[0] // BLOCK
    grid_keyval = project(norm_rows(grid_state, encode_grid_gain).astype(jnp.bfloat16), encode_keyval)
    mesh_query = project(norm_rows(mesh_state, encode_mesh_gain).astype(jnp.bfloat16), encode_query)
    owners = (encode_block // block_count).astype(jnp.int32)
    sorted_ids = jnp.argsort(owners, stable=True).astype(jnp.int32)
    counts = jnp.zeros((devices,), jnp.int32).at[owners].add(1)
    starts = (jnp.cumsum(counts) - counts).astype(jnp.int32)
    node_block = jnp.arange(MESH_DEV, dtype=jnp.int32) // BLOCK

    def encode(device):
        places = jnp.arange(slot_total, dtype=jnp.int32)
        filled = places < counts[device]
        row_ids = sorted_ids[jnp.minimum(starts[device] + places, grid_count - 1)]
        labels = jnp.where(filled, encode_block[row_ids] % block_count, -1).astype(jnp.int32)
        queries = lax.dynamic_slice_in_dim(mesh_query, (device * MESH_DEV).astype(jnp.int32), MESH_DEV, 0)
        return attend(queries, grid_keyval[row_ids], node_block[:, None] == labels[None, :])
    encoded = lax.map(encode, jnp.arange(devices, dtype=jnp.int32)).reshape(-1, features)
    mesh_mid = (mesh_state.astype(jnp.float32) + jnp.dot(encoded, encode_out, preferred_element_type=jnp.float32)).astype(jnp.bfloat16)
    mesh_qkv = project(norm_rows(mesh_mid, process_gain).astype(jnp.bfloat16), process_qkv)
    mesh_blocks = mesh_qkv.reshape(blocks_all, BLOCK, 3 * features)
    everywhere = jnp.ones((BLOCK, 2 * BLOCK), dtype=jnp.bool_)

    def process(index):
        own_rows = mesh_blocks[index]
        other_rows = mesh_blocks[neighbour_block[index]]
        key_rows = jnp.concatenate([own_rows[:, features:], other_rows[:, features:]], axis=0)
        return attend(own_rows[:, :features], key_rows, everywhere)
    processed = lax.map(process, jnp.arange(blocks_all, dtype=jnp.int32)).reshape(-1, features)
    mesh_out = (mesh_mid.astype(jnp.float32) + jnp.dot(processed, process_out, preferred_element_type=jnp.float32)).astype(jnp.bfloat16)
    grid_query = project(norm_rows(grid_state, decode_grid_gain).astype(jnp.bfloat16), decode_query)
    mesh_keyval = project(norm_rows(mesh_out, decode_mesh_gain).astype(jnp.bfloat16), decode_keyval).reshape(blocks_all, BLOCK, 2 * features)
    single_row = jnp.ones((1, BLOCK), dtype=jnp.bool_)

    def decode(start):
        queries = lax.dynamic_slice_in_dim(grid_query, start, BLOCK, 0)
        labels = lax.dynamic_slice_in_dim(decode_block, start, BLOCK, 0)
        key_rows = mesh_keyval[labels]
        return jax.vmap(lambda query_row, key_block: attend(query_row[None], key_block, single_row)[0])(queries, key_rows)
    decoded = lax.map(decode, jnp.arange(0, grid_count, BLOCK, dtype=jnp.int32)).reshape(-1, features)
    return jnp.dot(decoded, decode_out, preferred_element_type=jnp.float32).astype(jnp.bfloat16)
```

```python
import functools

import jax
import jax.numpy as jnp
from jax import lax
from jax.experimental import pallas as pl
from jax.experimental.pallas import tpu as pltpu
from jax.sharding import PartitionSpec as P

HEADS = 16
BLOCK = 128
TILE = 512
LANES = 128
MASKED = -1e30
AXES = ("gx", "gy")
F32 = jnp.float32
BF16 = jnp.bfloat16
MIB = 1024 * 1024


def iota(shape, dim):
    return lax.broadcasted_iota(jnp.int32, shape, dim)


def floor_div(values, by):
    return jnp.floor((values.astype(F32) + 0.5) * (1.0 / by)).astype(jnp.int32)


def dot(left, right):
    return jnp.dot(left, right, preferred_element_type=F32)


def dot_t(left, right):
    return lax.dot_general(left, right, (((1,), (1,)), ((), ())), preferred_element_type=F32)


def dot_tl(left, right):
    return lax.dot_general(left, right, (((0,), (0,)), ((), ())), preferred_element_type=F32)


def normed(values, gain):
    wide = values.astype(F32)
    return wide * lax.rsqrt(jnp.mean(wide * wide, axis=-1, keepdims=True) + 1e-06) * gain


def block_hits(blocks, total_blocks):
    hits = iota((total_blocks, blocks.shape[1]), 0) == blocks
    return jnp.where(hits, 1.0, 0.0).astype(F32)


def slots_of(hits, per_device, capacity):
    total_blocks, points = hits.shape
    earlier = jnp.where(iota((points, points), 0) < iota((points, points), 1), 1.0, 0.0)
    before = dot(hits.astype(BF16), earlier.astype(BF16))
    counts = jnp.broadcast_to(jnp.sum(hits, axis=1, keepdims=True), (total_blocks, LANES))
    row, column = iota((total_blocks, total_blocks), 0), iota((total_blocks, total_blocks), 1)
    mates = (floor_div(row, per_device) == floor_div(column, per_device)) & (column < row)
    offset = dot(jnp.where(mates, 1.0, 0.0).astype(BF16), counts.astype(BF16))[:, :1]
    owner = floor_div(iota((total_blocks, 1), 0), per_device)
    base = owner.astype(F32) * capacity + offset
    return jnp.sum(hits * (base + before), axis=0, keepdims=True).astype(jnp.int32)


def placement(slot, slots):
    return jnp.where(iota((slots, slot.shape[1]), 0) == slot, 1.0, 0.0).astype(BF16)


def fill_kernel(per_device, capacity, me_ref, state_ref, encode_ref, decode_ref, gain_ref, packed_ref, counts_ref):
    devices, wide = counts_ref.shape
    total_blocks = wide // 2
    encode_hits = block_hits(encode_ref[...], total_blocks)
    slot = slots_of(encode_hits, per_device, capacity)
    place = placement(slot, devices * capacity)
    norm = normed(state_ref[...], gain_ref[...]).astype(BF16)
    packed_ref[...] = dot(place, norm).astype(BF16)
    decode_hits = block_hits(decode_ref[...], total_blocks)
    both = jnp.concatenate([encode_hits, decode_hits], axis=0).astype(BF16)
    counts = dot_t(jnp.ones((8, both.shape[1]), BF16), both)[:1]
    counts_ref[...] = jnp.where(iota((devices, wide), 0) == me_ref[0], counts, 0.0)


def start_weights(weight, held, ready, base, count, first=0):
    @pl.loop(0, count)
    def _(i):
        columns = pl.ds(pl.multiple_of(first + i * TILE, TILE), TILE)
        pltpu.make_async_copy(weight.at[:, columns], held.at[base + i], ready.at[base + i]).start()


def with_weights(rows, weight, held, ready, base, count, put):
    @pl.loop(0, count)
    def _(i):
        pltpu.make_async_copy(
            weight.at[:, pl.ds(0, TILE)], held.at[base + i], ready.at[base + i]
        ).wait()
        put(pl.ds(pl.multiple_of(i * TILE, TILE), TILE), dot(rows[...], held[base + i]))


def store_in(ref):
    def put(columns, values):
        ref[:, columns] = values.astype(ref.dtype)

    return put


def query_kernel(
    per_device, capacity, total_blocks, scale,
    mesh_ref, mesh_gain, encode_query, grid_ref, grid_gain, decode_query, decode_ref,
    query_ref, packed_ref,
    norm_ref, held, ready,
):
    count = encode_query.shape[1] // TILE
    start_weights(decode_query, held, ready, 0, count)
    start_weights(encode_query, held, ready, count, count)
    norm_ref[...] = normed(grid_ref[...], grid_gain[...]).astype(BF16)
    slots = packed_ref.shape[0]
    slot = slots_of(block_hits(decode_ref[...], total_blocks), per_device, capacity)
    place = placement(slot, slots)

    def put_packed(columns, values):
        rounded = (values.astype(BF16).astype(F32) * scale).astype(BF16)
        packed_ref[:, columns] = dot(place, rounded).astype(BF16)

    with_weights(norm_ref, decode_query, held, ready, 0, count, put_packed)
    norm_ref[...] = normed(mesh_ref[...], mesh_gain[...]).astype(BF16)

    def put_query(columns, values):
        query_ref[:, columns] = (values.astype(BF16).astype(F32) * scale).astype(BF16)

    with_weights(norm_ref, encode_query, held, ready, count, count, put_query)


def own_counts(counts, me, per_device, first):
    wide = counts.shape[1]
    wanted = iota((8, wide), 1) == (iota((8, wide), 0) + (first + me * per_device))
    wanted = wanted & (iota((8, wide), 0) < per_device)
    return dot_t(jnp.where(wanted, 1.0, 0.0).astype(BF16), counts.astype(BF16)).astype(BF16)


def even_lanes(shape, head_size):
    return iota(shape, len(shape) - 1) < head_size


def split_heads(values, head_size):
    even = even_lanes(values.shape, head_size)
    zero = jnp.zeros_like(values)
    return jnp.concatenate([jnp.where(even, values, zero), jnp.where(even, zero, values)], axis=0)


def join_heads(values, head_size):
    rows = values.shape[0] // 2
    even = even_lanes((rows, values.shape[1]), head_size)
    return jnp.where(even, values[:rows], values[rows:])


def encode_kernel(
    per_device, capacity, head_size,
    me_ref, received_ref, counts_ref, query_ref, mesh_ref, gain_ref, keyval_w, out_w,
    mid_ref, norm_ref,
    keyval, attended, bias, held, ready,
):
    features = query_ref.shape[1]
    slots = received_ref.shape[0]
    devices = counts_ref.shape[0]
    kv_count, out_count = keyval_w.shape[1] // TILE, features // TILE
    start_weights(keyval_w, held, ready, 0, kv_count)
    start_weights(out_w, held, ready, kv_count, out_count)
    with_weights(received_ref, keyval_w, held, ready, 0, kv_count, store_in(keyval))

    mine = own_counts(counts_ref[...], me_ref[0], per_device, 0)
    sender = floor_div(iota((devices, slots), 1), capacity) == iota((devices, slots), 0)
    filled = dot(mine, jnp.where(sender, 1.0, 0.0).astype(BF16))
    lane = iota((1, slots), 1)
    place = (lane - floor_div(lane, capacity) * capacity).astype(F32)
    begin = jnp.zeros((1, slots), F32)
    for block in range(per_device):
        end = begin + filled[block : block + 1]
        bias[block : block + 1] = jnp.where((place >= begin) & (place < end), 0.0, MASKED)
        begin = end

    @pl.loop(0, features // LANES)
    def _(pair):
        columns = pl.ds(pl.multiple_of(pair * LANES, LANES), LANES)
        value_columns = pl.ds(pl.multiple_of(features + pair * LANES, LANES), LANES)
        keys, values = keyval[:, columns], keyval[:, value_columns]
        for block in range(per_device):
            rows = pl.ds(block * BLOCK, BLOCK)
            queries = split_heads(query_ref[rows, columns], head_size)
            scores = dot_t(queries, keys) + bias[block : block + 1]
            powers = jnp.exp(scores - jnp.max(scores, axis=-1, keepdims=True))
            sums = jnp.sum(powers, axis=-1, keepdims=True)
            output = dot(powers.astype(BF16), values) / sums
            attended[rows, columns] = join_heads(output, head_size).astype(BF16)

    def put_mid(columns, values):
        mid_ref[:, columns] = (mesh_ref[:, columns].astype(F32) + values).astype(BF16)

    with_weights(attended, out_w, held, ready, kv_count, out_count, put_mid)
    norm_ref[...] = normed(mid_ref[...], gain_ref[...]).astype(BF16)


def process_kernel(
    per_device, capacity, head_size, scale,
    me_ref, position_ref, counts_ref, qkv_ref, before_ref, norm_ref, after_ref, mid_ref, queries_ref, gain_ref,
    qkv_w, out_w, decode_w,
    answers_ref,
    chosen, other, attended, mesh_out, held, ready,
):
    features = mid_ref.shape[1]
    slots, devices = queries_ref.shape[0], counts_ref.shape[0]
    kv_count, out_count = 2 * features // TILE, features // TILE
    start_weights(qkv_w, held, ready, 0, kv_count, features)
    start_weights(out_w, held, ready, kv_count, out_count)
    start_weights(decode_w, held, ready, kv_count + out_count, kv_count)
    for block in range(per_device):
        rows = pl.ds(block * BLOCK, BLOCK)
        position = position_ref[block]
        for side, source in enumerate((before_ref, norm_ref, after_ref)):
            for place in range(per_device):
                @pl.when(position == side * per_device + place)
                def _():
                    chosen[rows] = source[pl.ds(place * BLOCK, BLOCK)]

    with_weights(chosen, qkv_w, held, ready, 0, kv_count, store_in(other))

    @pl.loop(0, features // LANES)
    def _(pair):
        columns = pl.ds(pl.multiple_of(pair * LANES, LANES), LANES)
        second = pl.ds(pl.multiple_of(features + pair * LANES, LANES), LANES)
        third = pl.ds(pl.multiple_of(2 * features + pair * LANES, LANES), LANES)
        for block in range(per_device):
            rows = pl.ds(block * BLOCK, BLOCK)
            queries = split_heads((qkv_ref[rows, columns].astype(F32) * scale).astype(BF16), head_size)
            keys = jnp.concatenate([qkv_ref[rows, second], other[rows, columns]], axis=0)
            values = jnp.concatenate([qkv_ref[rows, third], other[rows, second]], axis=0)
            scores = dot_t(queries, keys)
            powers = jnp.exp(scores - jnp.max(scores, axis=-1, keepdims=True))
            sums = jnp.sum(powers, axis=-1, keepdims=True)
            output = dot(powers.astype(BF16), values) / sums
            attended[rows, columns] = join_heads(output, head_size).astype(BF16)

    def put_out(columns, values):
        mesh_out[:, columns] = (mid_ref[:, columns].astype(F32) + values).astype(BF16)

    with_weights(attended, out_w, held, ready, kv_count, out_count, put_out)
    chosen[...] = normed(mesh_out[...], gain_ref[...]).astype(BF16)
    with_weights(chosen, decode_w, held, ready, kv_count + out_count, kv_count, store_in(other))

    total_blocks = counts_ref.shape[1] // 2
    mine = own_counts(counts_ref[...], me_ref[0], per_device, total_blocks)
    sender = floor_div(iota((slots, devices), 0), capacity) == iota((slots, devices), 1)
    filled = dot_t(jnp.where(sender, 1.0, 0.0).astype(BF16), mine)
    row = iota((slots, 1), 0)
    place = (row - floor_div(row, capacity) * capacity).astype(F32)
    reads, begin = [], jnp.zeros((slots, 1), F32)
    for block in range(per_device):
        end = begin + filled[:, block : block + 1]
        reads.append(jnp.broadcast_to(jnp.where((place >= begin) & (place < end), 1.0, 0.0), (slots, BLOCK)))
        begin = end

    @pl.loop(0, features // LANES)
    def _(pair):
        columns = pl.ds(pl.multiple_of(pair * LANES, LANES), LANES)
        second = pl.ds(pl.multiple_of(features + pair * LANES, LANES), LANES)
        queries = queries_ref[:, columns]
        even = even_lanes((slots, LANES), head_size)
        outputs = []
        for head in range(LANES // head_size):
            picked = jnp.where(even if head == 0 else ~even, queries, jnp.zeros_like(queries))
            scores = dot_t(picked, other[:, columns])
            chosen_scores = scores[:, :BLOCK]
            for block in range(1, per_device):
                here = scores[:, block * BLOCK : (block + 1) * BLOCK]
                chosen_scores = jnp.where(reads[block] > 0.5, here, chosen_scores)
            powers = jnp.exp(chosen_scores - jnp.max(chosen_scores, axis=-1, keepdims=True))
            sums = jnp.sum(powers, axis=-1, keepdims=True)
            spread = jnp.concatenate(
                [jnp.where(reads[block] > 0.5, powers, 0.0).astype(BF16) for block in range(per_device)], axis=1
            )
            outputs.append(dot(spread, other[:, second]) / sums)
        answers_ref[:, columns] = jnp.where(even, outputs[0], outputs[1]).astype(BF16)


def unpack_kernel(
    per_device, capacity, total_blocks, replies_ref, decode_ref, out_w, update_ref, decoded, held, ready
):
    count = out_w.shape[1] // TILE
    start_weights(out_w, held, ready, 0, count)
    slot = slots_of(block_hits(decode_ref[...], total_blocks), per_device, capacity)
    place = placement(slot, replies_ref.shape[0])
    decoded[...] = dot_tl(place, replies_ref[...]).astype(BF16)
    with_weights(decoded, out_w, held, ready, 0, count, store_in(update_ref))


VMEM, SMEM, ANY = pltpu.VMEM, pltpu.SMEM, pl.ANY


def call(kernel, operands, outs, scratch, name, limit, flops=0):
    spaces = [space for space, _ in operands]
    return pl.pallas_call(
        kernel,
        out_shape=[jax.ShapeDtypeStruct(shape, kind) for shape, kind in outs],
        in_specs=[pl.BlockSpec(memory_space=space) for space in spaces],
        out_specs=[pl.BlockSpec(memory_space=VMEM) for _ in outs],
        scratch_shapes=scratch,
        name=name,
        cost_estimate=pl.CostEstimate(flops=flops, bytes_accessed=4 * MIB, transcendentals=0),
        compiler_params=pltpu.CompilerParams(vmem_limit_bytes=limit * MIB),
    )(*[value for _, value in operands])


def weights_held(count, features):
    return [VMEM((count, features, TILE), BF16), pltpu.SemaphoreType.DMA((count,))]


def on_device(
    grid_state,
    mesh_state,
    encode_block,
    neighbour_block,
    decode_block,
    encode_grid_gain,
    encode_mesh_gain,
    process_gain,
    decode_grid_gain,
    decode_mesh_gain,
    encode_query,
    encode_keyval,
    encode_out,
    process_qkv,
    process_out,
    decode_query,
    decode_keyval,
    decode_out,
):
    devices = lax.axis_size(AXES)
    me = lax.axis_index(AXES)
    grid_count, features = grid_state.shape
    mesh_rows = mesh_state.shape[0]
    per_device = mesh_rows // BLOCK
    total_blocks = per_device * devices
    capacity = max(4, 2 * grid_count // devices)
    slots = devices * capacity
    head_size = features // HEADS
    scale = head_size ** (-0.5)
    tiles = features // TILE
    me_row = me.astype(jnp.int32).reshape(1)
    position = neighbour_block - me * per_device + per_device
    encode_row, decode_row = encode_block.reshape(1, -1), decode_block.reshape(1, -1)
    gains = [
        gain.reshape(1, -1)
        for gain in (encode_grid_gain, encode_mesh_gain, process_gain, decode_grid_gain, decode_mesh_gain)
    ]

    def exchange(rows):
        return lax.all_to_all(
            rows.reshape(devices, capacity, features), AXES, split_axis=0, concat_axis=0, tiled=True
        ).reshape(slots, features)

    packed, counts = call(
        functools.partial(fill_kernel, per_device, capacity),
        [(SMEM, me_row), (VMEM, grid_state), (VMEM, encode_row), (VMEM, decode_row), (VMEM, gains[0])],
        [((slots, features), BF16), ((devices, 2 * total_blocks), F32)],
        [],
        "fill",
        32,
        flops=600_000_000,
    )
    received = exchange(packed)
    step = 1
    while step < devices:
        counts = counts + lax.ppermute(counts, AXES, [(i, i ^ step) for i in range(devices)])
        step *= 2
    query, packed_queries = call(
        functools.partial(query_kernel, per_device, capacity, total_blocks, scale),
        [
            (VMEM, mesh_state), (VMEM, gains[1]), (ANY, encode_query),
            (VMEM, grid_state), (VMEM, gains[3]), (ANY, decode_query), (VMEM, decode_row),
        ],
        [((mesh_rows, features), BF16), ((slots, features), BF16)],
        [VMEM((grid_count, features), BF16), *weights_held(2 * tiles, features)],
        "queries",
        32,
        flops=2_000_000_000,
    )
    arrived_queries = exchange(packed_queries)
    mesh_mid, process_norm = call(
        functools.partial(encode_kernel, per_device, capacity, head_size),
        [
            (SMEM, me_row), (VMEM, received), (VMEM, counts), (VMEM, query), (VMEM, mesh_state), (VMEM, gains[2]),
            (ANY, encode_keyval), (ANY, encode_out),
        ],
        [((mesh_rows, features), BF16), ((mesh_rows, features), BF16)],
        [
            VMEM((slots, 2 * features), BF16),
            VMEM((mesh_rows, features), BF16),
            VMEM((8, slots), F32),
            *weights_held(3 * tiles, features),
        ],
        "encode",
        32,
        flops=5_000_000_000,
    )
    before = lax.ppermute(process_norm, AXES, [(i, i + 1) for i in range(devices - 1)])
    after = lax.ppermute(process_norm, AXES, [(i + 1, i) for i in range(devices - 1)])
    mesh_qkv = dot(process_norm, process_qkv).astype(BF16)
    (answers,) = call(
        functools.partial(process_kernel, per_device, capacity, head_size, scale),
        [
            (SMEM, me_row), (SMEM, position), (VMEM, counts), (VMEM, mesh_qkv), (VMEM, before), (VMEM, process_norm),
            (VMEM, after), (VMEM, mesh_mid), (VMEM, arrived_queries), (VMEM, gains[4]),
            (ANY, process_qkv), (ANY, process_out), (ANY, decode_keyval),
        ],
        [((slots, features), BF16)],
        [
            VMEM((mesh_rows, features), BF16),
            VMEM((mesh_rows, 2 * features), BF16),
            VMEM((mesh_rows, features), BF16),
            VMEM((mesh_rows, features), BF16),
            *weights_held(5 * tiles, features),
        ],
        "process",
        40,
        flops=6_000_000_000,
    )
    replies = exchange(answers)
    (update,) = call(
        functools.partial(unpack_kernel, per_device, capacity, total_blocks),
        [(VMEM, replies), (VMEM, decode_row), (ANY, decode_out)],
        [((grid_count, features), BF16)],
        [VMEM((grid_count, features), BF16), *weights_held(tiles, features)],
        "unpack",
        32,
        flops=1_000_000_000,
    )
    return update


def solution(mesh):
    in_specs = (P(AXES, None), P(AXES, None), P(AXES), P(AXES), P(AXES), *[P()] * 13)
    return jax.shard_map(
        on_device, mesh=mesh, in_specs=in_specs, out_specs=P(AXES, None), check_vma=False
    )
```

```python
import functools

import jax
import jax.numpy as jnp
from jax import lax
from jax.experimental import pallas as pl
from jax.experimental.pallas import tpu as pltpu
from jax.sharding import PartitionSpec as P

HEADS = 16
BLOCK = 128
TILE = 512
LANES = 128
MASKED = -1e30
VMEM_MIB = 62
ENCODE_UNROLL = 1
PROCESS_UNROLL = 1
ANY, HBM, VMEM, SMEM = pl.ANY, pltpu.HBM, pltpu.VMEM, pltpu.SMEM
AXES = ("gx", "gy")
F32 = jnp.float32
BF16 = jnp.bfloat16
MIB = 1024 * 1024


def iota(shape, dim):
    return lax.broadcasted_iota(jnp.int32, shape, dim)


def floor_div(values, by):
    return jnp.floor((values.astype(F32) + 0.5) * (1.0 / by)).astype(jnp.int32)


def dot(left, right):
    return jnp.dot(left, right, preferred_element_type=F32)


def dot_t(left, right):
    return lax.dot_general(left, right, (((1,), (1,)), ((), ())), preferred_element_type=F32)


def dot_tl(left, right):
    return lax.dot_general(left, right, (((0,), (0,)), ((), ())), preferred_element_type=F32)


def normed(values, gain):
    wide = values.astype(F32)
    return wide * lax.rsqrt(jnp.mean(wide * wide, axis=-1, keepdims=True) + 1e-06) * gain


def block_hits(blocks, total_blocks):
    hits = iota((total_blocks, blocks.shape[1]), 0) == blocks
    return jnp.where(hits, 1.0, 0.0).astype(F32)


def block_counts(hits):
    counts = jnp.sum(hits, axis=1, keepdims=True)
    return jnp.broadcast_to(counts, (hits.shape[0], LANES)).astype(BF16)


def slots_of(hits, per_device, capacity):
    total_blocks, points = hits.shape
    earlier = jnp.where(iota((points, points), 0) < iota((points, points), 1), 1.0, 0.0)
    before = dot(hits.astype(BF16), earlier.astype(BF16))
    row, column = iota((total_blocks, total_blocks), 0), iota((total_blocks, total_blocks), 1)
    mates = (floor_div(row, per_device) == floor_div(column, per_device)) & (column < row)
    offset = dot(jnp.where(mates, 1.0, 0.0).astype(BF16), block_counts(hits))[:, :1]
    owner = floor_div(iota((total_blocks, 1), 0), per_device)
    base = owner.astype(F32) * capacity + offset
    return jnp.sum(hits * (base + before), axis=0, keepdims=True).astype(jnp.int32)


def placement(slot, slots):
    return jnp.where(iota((slots, slot.shape[1]), 0) == slot, 1.0, 0.0).astype(BF16)


class Fetch:
    def __init__(self, source, held, ready):
        self.copy = pltpu.make_async_copy(source, held, ready)
        self.held = held
        self.waiting = True
        self.copy.start()

    def __call__(self):
        if self.waiting:
            self.copy.wait()
            self.waiting = False
        return self.held


class Weight:
    def __init__(self, source, held, ready, base, count, first=0):
        self.source, self.held, self.ready, self.base, self.count = source, held, ready, base, count

        @pl.loop(0, count)
        def _(i):
            columns = pl.ds(pl.multiple_of((first + i) * TILE, TILE), TILE)
            pltpu.make_async_copy(source.at[:, columns], held.at[base + i], ready.at[base + i]).start()

    def product(self, rows, put):
        @pl.loop(0, self.count)
        def _(i):
            held = self.held.at[self.base + i]
            pltpu.make_async_copy(
                self.source.at[:, pl.ds(0, TILE)], held, self.ready.at[self.base + i]
            ).wait()
            put(pl.ds(pl.multiple_of(i * TILE, TILE), TILE), dot(rows[...], held[...]))


def store_in(ref):
    def put(columns, values):
        ref[:, columns] = values.astype(ref.dtype)

    return put


def count_lanes(encode_counts, decode_counts, devices, per_device):
    total_blocks = encode_counts.shape[0]
    lane = iota((devices, LANES), 1)
    labels = jnp.zeros((devices, LANES), F32)
    for kind, counts in enumerate((encode_counts, decode_counts)):
        for block in range(per_device):
            wanted = iota((devices, total_blocks), 0) * per_device + block
            wanted = jnp.where(iota((devices, total_blocks), 1) == wanted, 1.0, 0.0).astype(BF16)
            labels = labels + jnp.where(lane == kind * per_device + block, dot(wanted, counts), 0.0)
    return labels.astype(BF16)


def by_tiles(capacity):
    return capacity % 16 == 0


def fill_kernel(
    devices, per_device, capacity,
    state_hbm, encode_hbm, decode_hbm, gain_hbm, packed_ref,
    state_held, encode_held, decode_held, gain_held, ready,
):
    encode = Fetch(encode_hbm, encode_held, ready.at[0])
    decode = Fetch(decode_hbm, decode_held, ready.at[1])
    state = Fetch(state_hbm, state_held, ready.at[2])
    gain = Fetch(gain_hbm, gain_held, ready.at[3])
    total_blocks, slots = devices * per_device, devices * capacity
    encode_hits = block_hits(encode()[...], total_blocks)
    place = placement(slots_of(encode_hits, per_device, capacity), slots)
    decode_hits = block_hits(decode()[...], total_blocks)
    labels = count_lanes(block_counts(encode_hits), block_counts(decode_hits), devices, per_device)
    norm = normed(state()[...], gain()[...]).astype(BF16)
    features = norm.shape[1]
    if by_tiles(capacity):
        for tile in range(features // LANES):
            columns = dot(place, norm[:, tile * LANES : (tile + 1) * LANES]).astype(BF16)
            packed_ref[:, pl.ds(tile * capacity, capacity), :] = columns.reshape(devices, capacity, LANES)
        last = pl.ds(features // LANES * capacity, 8)
        packed_ref[:, last, :] = jnp.broadcast_to(labels[:, None, :], (devices, 8, LANES))
    else:
        packed_ref[:, pl.ds(0, features)] = dot(place, norm).astype(BF16)
        owner = floor_div(iota((slots, devices), 0), capacity) == iota((slots, devices), 1)
        packed_ref[:, pl.ds(features, LANES)] = dot(jnp.where(owner, 1.0, 0.0).astype(BF16), labels).astype(BF16)


def query_kernel(
    devices, per_device, capacity, scale,
    mesh_hbm, mesh_gain_hbm, encode_w, grid_hbm, grid_gain_hbm, decode_w, decode_hbm,
    query_ref, packed_ref,
    mesh_held, mesh_gain_held, grid_held, grid_gain_held, decode_held, ready,
    norm_ref, weights, arrived,
):
    decode = Fetch(decode_hbm, decode_held, ready.at[0])
    grid = Fetch(grid_hbm, grid_held, ready.at[1])
    grid_gain = Fetch(grid_gain_hbm, grid_gain_held, ready.at[2])
    mesh = Fetch(mesh_hbm, mesh_held, ready.at[3])
    mesh_gain = Fetch(mesh_gain_hbm, mesh_gain_held, ready.at[4])
    count = encode_w.shape[1] // TILE
    decode_weight = Weight(decode_w, weights, arrived, 0, count)
    encode_weight = Weight(encode_w, weights, arrived, count, count)
    slots = packed_ref.shape[0]
    hits = block_hits(decode()[...], devices * per_device)
    place = placement(slots_of(hits, per_device, capacity), slots)
    norm_ref[...] = normed(grid()[...], grid_gain()[...]).astype(BF16)

    def put_packed(columns, values):
        rounded = (values.astype(BF16).astype(F32) * scale).astype(BF16)
        packed_ref[:, columns] = dot(place, rounded).astype(BF16)

    decode_weight.product(norm_ref, put_packed)
    norm_ref[...] = normed(mesh()[...], mesh_gain()[...]).astype(BF16)

    def put_query(columns, values):
        query_ref[:, columns] = (values.astype(BF16).astype(F32) * scale).astype(BF16)

    encode_weight.product(norm_ref, put_query)


def lanes_of(labels, first, count):
    row, lane = iota((8, LANES), 0), iota((8, LANES), 1)
    wanted = (lane == row + first) & (row < count)
    return dot_t(jnp.where(wanted, 1.0, 0.0).astype(BF16), labels).astype(BF16)


def even_lanes(shape, head_size):
    return iota(shape, len(shape) - 1) < head_size


def split_heads(values, head_size):
    even = even_lanes(values.shape, head_size)
    zero = jnp.zeros_like(values)
    return jnp.concatenate([jnp.where(even, values, zero), jnp.where(even, zero, values)], axis=0)


def join_heads(values, head_size):
    rows = values.shape[0] // 2
    even = even_lanes((rows, values.shape[1]), head_size)
    return jnp.where(even, values[:rows], values[rows:])


def encode_kernel(
    per_device, capacity, head_size, unroll,
    received_hbm, query_hbm, mesh_hbm, gain_hbm, keyval_w, out_w,
    mid_ref, norm_ref, labels_ref,
    received_held, query_held, mesh_held, gain_held, ready,
    rows_ref, keyval, attended, bias, weights, arrived,
):
    features = mid_ref.shape[1]
    devices = labels_ref.shape[0]
    slots = devices * capacity
    kv_count, out_count = keyval_w.shape[1] // TILE, features // TILE
    received = Fetch(received_hbm, received_held, ready.at[0])
    keyval_weight = Weight(keyval_w, weights, arrived, 0, kv_count)
    query_rows = Fetch(query_hbm, query_held, ready.at[1])
    out_weight = Weight(out_w, weights, arrived, kv_count, out_count)
    mesh = Fetch(mesh_hbm, mesh_held, ready.at[2])
    gain = Fetch(gain_hbm, gain_held, ready.at[3])
    received_ref = received()
    if by_tiles(capacity):
        for tile in range(features // LANES):
            part = received_ref[:, pl.ds(tile * capacity, capacity), :]
            rows_ref[:, pl.ds(tile * LANES, LANES)] = part.reshape(slots, LANES)
        last = received_ref[:, pl.ds(features // LANES * capacity, 8), :]
        labels = jnp.max(last.astype(F32), axis=1).astype(BF16)
        rows = rows_ref
    else:
        rows = received_ref.at[:, pl.ds(0, features)]
        first = iota((devices, slots), 1) == iota((devices, slots), 0) * capacity
        labels = dot(jnp.where(first, 1.0, 0.0).astype(BF16), received_ref[:, pl.ds(features, LANES)]).astype(BF16)
    labels_ref[...] = labels
    keyval_weight.product(rows, store_in(keyval))

    sender = floor_div(iota((devices, slots), 1), capacity) == iota((devices, slots), 0)
    filled = dot(lanes_of(labels, 0, per_device), jnp.where(sender, 1.0, 0.0).astype(BF16))
    lane = iota((1, slots), 1)
    place = (lane - floor_div(lane, capacity) * capacity).astype(F32)
    begin = jnp.zeros((1, slots), F32)
    for block in range(per_device):
        end = begin + filled[block : block + 1]
        bias[block : block + 1] = jnp.where((place >= begin) & (place < end), 0.0, MASKED)
        begin = end
    query_ref = query_rows()

    @pl.loop(0, features // LANES, unroll=unroll)
    def _(pair):
        columns = pl.ds(pl.multiple_of(pair * LANES, LANES), LANES)
        value_columns = pl.ds(pl.multiple_of(features + pair * LANES, LANES), LANES)
        keys, values = keyval[:, columns], keyval[:, value_columns]
        for block in range(per_device):
            block_rows = pl.ds(block * BLOCK, BLOCK)
            queries = split_heads(query_ref[block_rows, columns], head_size)
            scores = dot_t(queries, keys) + bias[block : block + 1]
            powers = jnp.exp(scores - jnp.max(scores, axis=-1, keepdims=True))
            sums = jnp.sum(powers, axis=-1, keepdims=True)
            output = dot(powers.astype(BF16), values) / sums
            attended[block_rows, columns] = join_heads(output, head_size).astype(BF16)

    mesh_ref = mesh()

    def put_mid(columns, values):
        mid_ref[:, columns] = (mesh_ref[:, columns].astype(F32) + values).astype(BF16)

    out_weight.product(attended, put_mid)
    norm_ref[...] = normed(mid_ref[...], gain()[...]).astype(BF16)


def own_kernel(scale, norm_hbm, qkv_w, qkv_ref, norm_held, ready, weights, arrived):
    features = norm_hbm.shape[1]
    norm = Fetch(norm_hbm, norm_held, ready.at[0])
    weight = Weight(qkv_w, weights, arrived, 0, qkv_w.shape[1] // TILE)
    tiles = features // TILE

    def put(columns, values):
        qkv_ref[:, columns] = values.astype(BF16)

    weight.product(norm(), put)
    queries = pl.ds(0, features)
    qkv_ref[:, queries] = (qkv_ref[:, queries].astype(F32) * scale).astype(BF16)


def process_kernel(
    per_device, capacity, head_size, unroll,
    me_ref, position_ref, first_hbm, norm_hbm, second_hbm, qkv_hbm, mid_hbm, queries_hbm, gain_hbm, labels_hbm,
    qkv_w, out_w, decode_w,
    answers_ref,
    qkv_held, mid_held, queries_held, gain_held, labels_held, ready, picked,
    chosen, other, attended, mesh_out, weights, arrived,
):
    features = mid_hbm.shape[1]
    slots, devices = queries_hbm.shape[0], labels_hbm.shape[0]
    tiles = features // TILE
    odd = me_ref[0] % 2
    for block in range(per_device):
        rows = pl.ds(block * BLOCK, BLOCK)
        position = position_ref[block]
        sides = ((first_hbm, 2 * (1 - odd)), (norm_hbm, 1), (second_hbm, 2 * odd))
        for source, side in sides:
            for place in range(per_device):
                @pl.when(position == side * per_device + place)
                def _():
                    block_rows = source.at[pl.ds(place * BLOCK, BLOCK)]
                    pltpu.make_async_copy(block_rows, chosen.at[rows], picked.at[block]).start()

    kv_weight = Weight(qkv_w, weights, arrived, 0, 2 * tiles, tiles)
    out_weight = Weight(out_w, weights, arrived, 2 * tiles, tiles)
    decode_weight = Weight(decode_w, weights, arrived, 3 * tiles, 2 * tiles)
    qkv = Fetch(qkv_hbm, qkv_held, ready.at[0])
    mid = Fetch(mid_hbm, mid_held, ready.at[1])
    queries_rows = Fetch(queries_hbm, queries_held, ready.at[2])
    gain = Fetch(gain_hbm, gain_held, ready.at[3])
    labels = Fetch(labels_hbm, labels_held, ready.at[4])
    for block in range(per_device):
        rows = pl.ds(block * BLOCK, BLOCK)
        pltpu.make_async_copy(norm_hbm.at[rows], chosen.at[rows], picked.at[block]).wait()
    kv_weight.product(chosen, store_in(other))
    qkv_ref = qkv()

    @pl.loop(0, features // LANES, unroll=unroll)
    def _(pair):
        columns = pl.ds(pl.multiple_of(pair * LANES, LANES), LANES)
        second = pl.ds(pl.multiple_of(features + pair * LANES, LANES), LANES)
        third = pl.ds(pl.multiple_of(2 * features + pair * LANES, LANES), LANES)
        for block in range(per_device):
            rows = pl.ds(block * BLOCK, BLOCK)
            queries = split_heads(qkv_ref[rows, columns], head_size)
            keys = jnp.concatenate([qkv_ref[rows, second], other[rows, columns]], axis=0)
            values = jnp.concatenate([qkv_ref[rows, third], other[rows, second]], axis=0)
            scores = dot_t(queries, keys)
            powers = jnp.exp(scores - jnp.max(scores, axis=-1, keepdims=True))
            sums = jnp.sum(powers, axis=-1, keepdims=True)
            output = dot(powers.astype(BF16), values) / sums
            attended[rows, columns] = join_heads(output, head_size).astype(BF16)

    mid_ref = mid()

    def put_out(columns, values):
        mesh_out[:, columns] = (mid_ref[:, columns].astype(F32) + values).astype(BF16)

    out_weight.product(attended, put_out)
    chosen[...] = normed(mesh_out[...], gain()[...]).astype(BF16)
    decode_weight.product(chosen, store_in(other))

    sender = floor_div(iota((slots, devices), 0), capacity) == iota((slots, devices), 1)
    filled = dot_t(jnp.where(sender, 1.0, 0.0).astype(BF16), lanes_of(labels()[...], per_device, per_device))
    row = iota((slots, 1), 0)
    place = (row - floor_div(row, capacity) * capacity).astype(F32)
    reads, begin = [], jnp.zeros((slots, 1), F32)
    for block in range(per_device):
        end = begin + filled[:, block : block + 1]
        here = jnp.where((place >= begin) & (place < end), 1.0, 0.0)
        reads.append(jnp.broadcast_to(here, (slots, BLOCK)))
        begin = end
    queries_ref = queries_rows()

    @pl.loop(0, features // LANES, unroll=unroll)
    def _(pair):
        columns = pl.ds(pl.multiple_of(pair * LANES, LANES), LANES)
        second = pl.ds(pl.multiple_of(features + pair * LANES, LANES), LANES)
        queries = queries_ref[:, columns]
        even = even_lanes((slots, LANES), head_size)
        outputs = []
        for head in range(LANES // head_size):
            picked = jnp.where(even if head == 0 else ~even, queries, jnp.zeros_like(queries))
            scores = dot_t(picked, other[:, columns])
            chosen_scores = scores[:, :BLOCK]
            for block in range(1, per_device):
                here = scores[:, block * BLOCK : (block + 1) * BLOCK]
                chosen_scores = jnp.where(reads[block] > 0.5, here, chosen_scores)
            powers = jnp.exp(chosen_scores - jnp.max(chosen_scores, axis=-1, keepdims=True))
            sums = jnp.sum(powers, axis=-1, keepdims=True)
            spread = jnp.concatenate(
                [jnp.where(reads[block] > 0.5, powers, 0.0).astype(BF16) for block in range(per_device)], axis=1
            )
            outputs.append(dot(spread, other[:, second]) / sums)
        answers_ref[:, columns] = jnp.where(even, outputs[0], outputs[1]).astype(BF16)


def unpack_kernel(
    devices, per_device, capacity, replies_hbm, decode_hbm, out_w, update_ref,
    decode_held, replies_held, ready, decoded, weights, arrived,
):
    decode = Fetch(decode_hbm, decode_held, ready.at[0])
    replies = Fetch(replies_hbm, replies_held, ready.at[1])
    weight = Weight(out_w, weights, arrived, 0, out_w.shape[1] // TILE)
    hits = block_hits(decode()[...], devices * per_device)
    place = placement(slots_of(hits, per_device, capacity), replies_hbm.shape[0])
    decoded[...] = dot_tl(place, replies()[...]).astype(BF16)
    weight.product(decoded, store_in(update_ref))


def call(kernel, operands, outs, scratch, name, flops):
    return pl.pallas_call(
        kernel,
        out_shape=[jax.ShapeDtypeStruct(shape, kind) for shape, kind in outs],
        in_specs=[pl.BlockSpec(memory_space=space) for space, _ in operands],
        out_specs=[pl.BlockSpec(memory_space=VMEM) for _ in outs],
        scratch_shapes=scratch,
        name=name,
        cost_estimate=pl.CostEstimate(flops=flops, bytes_accessed=4 * MIB, transcendentals=0),
        compiler_params=pltpu.CompilerParams(vmem_limit_bytes=VMEM_MIB * MIB),
    )(*[value for _, value in operands])


def held_like(*values):
    return [*[VMEM(value.shape, value.dtype) for value in values], pltpu.SemaphoreType.DMA((len(values),))]


def weights_held(count, features):
    return [VMEM((count, features, TILE), BF16), pltpu.SemaphoreType.DMA((count,))]


def on_device(
    grid_state,
    mesh_state,
    encode_block,
    neighbour_block,
    decode_block,
    encode_grid_gain,
    encode_mesh_gain,
    process_gain,
    decode_grid_gain,
    decode_mesh_gain,
    encode_query,
    encode_keyval,
    encode_out,
    process_qkv,
    process_out,
    decode_query,
    decode_keyval,
    decode_out,
):
    devices = lax.axis_size(AXES)
    me = lax.axis_index(AXES)
    grid_count, features = grid_state.shape
    mesh_rows = mesh_state.shape[0]
    per_device = mesh_rows // BLOCK
    total_blocks = per_device * devices
    capacity = max(4, 2 * grid_count // devices)
    slots = devices * capacity
    head_size = features // HEADS
    scale = head_size ** (-0.5)
    tiles = features // TILE
    me_row = me.astype(jnp.int32).reshape(1)
    position = neighbour_block - me * per_device + per_device
    encode_row, decode_row = encode_block.reshape(1, -1), decode_block.reshape(1, -1)
    encode_grid_gain, encode_mesh_gain, process_gain, decode_grid_gain, decode_mesh_gain = [
        gain.reshape(1, -1)
        for gain in (encode_grid_gain, encode_mesh_gain, process_gain, decode_grid_gain, decode_mesh_gain)
    ]

    def exchange(rows, *shape):
        return lax.all_to_all(rows.reshape(devices, *shape), AXES, split_axis=0, concat_axis=0, tiled=True)

    if by_tiles(capacity):
        payload = (capacity * features // LANES + 8, LANES)
        packed_shape = (devices, *payload)
    else:
        payload = (capacity, features + LANES)
        packed_shape = (slots, features + LANES)
    (packed,) = call(
        functools.partial(fill_kernel, devices, per_device, capacity),
        [(HBM, grid_state), (HBM, encode_row), (HBM, decode_row), (HBM, encode_grid_gain)],
        [(packed_shape, BF16)],
        held_like(grid_state, encode_row, decode_row, encode_grid_gain),
        "fill",
        flops=600_000_000,
    )
    received = exchange(packed, *payload).reshape(packed_shape)
    query, packed_queries = call(
        functools.partial(query_kernel, devices, per_device, capacity, scale),
        [
            (HBM, mesh_state), (HBM, encode_mesh_gain), (HBM, encode_query),
            (HBM, grid_state), (HBM, decode_grid_gain), (HBM, decode_query), (HBM, decode_row),
        ],
        [((mesh_rows, features), BF16), ((slots, features), BF16)],
        [
            *held_like(mesh_state, encode_mesh_gain, grid_state, decode_grid_gain, decode_row),
            VMEM((grid_count, features), BF16),
            *weights_held(2 * tiles, features),
        ],
        "queries",
        flops=2_000_000_000,
    )
    arrived_queries = exchange(packed_queries, capacity, features).reshape(slots, features)
    mesh_mid, process_norm, labels = call(
        functools.partial(encode_kernel, per_device, capacity, head_size, ENCODE_UNROLL),
        [
            (ANY, received), (HBM, query), (HBM, mesh_state), (HBM, process_gain),
            (HBM, encode_keyval), (HBM, encode_out),
        ],
        [((mesh_rows, features), BF16), ((mesh_rows, features), BF16), ((devices, LANES), BF16)],
        [
            *held_like(received, query, mesh_state, process_gain),
            VMEM((slots, features), BF16),
            VMEM((slots, 2 * features), BF16),
            VMEM((mesh_rows, features), BF16),
            VMEM((8, slots), F32),
            *weights_held(3 * tiles, features),
        ],
        "encode",
        flops=5_000_000_000,
    )
    pairs = [(i, i ^ 1) for i in range(devices)]
    across = [(i, i + 1 if i % 2 else i - 1) for i in range(1, devices - 1)]
    first = lax.ppermute(process_norm, AXES, pairs)
    second = lax.ppermute(process_norm, AXES, across)
    (mesh_qkv,) = call(
        functools.partial(own_kernel, scale),
        [(HBM, process_norm), (HBM, process_qkv)],
        [((mesh_rows, 3 * features), BF16)],
        [*held_like(process_norm), *weights_held(3 * tiles, features)],
        "own",
        flops=2_000_000_000,
    )
    (answers,) = call(
        functools.partial(process_kernel, per_device, capacity, head_size, PROCESS_UNROLL),
        [
            (SMEM, me_row), (SMEM, position), (ANY, first), (HBM, process_norm), (ANY, second), (HBM, mesh_qkv),
            (HBM, mesh_mid), (ANY, arrived_queries), (HBM, decode_mesh_gain), (HBM, labels),
            (HBM, process_qkv), (HBM, process_out), (HBM, decode_keyval),
        ],
        [((slots, features), BF16)],
        [
            *held_like(mesh_qkv, mesh_mid, arrived_queries, decode_mesh_gain, labels),
            pltpu.SemaphoreType.DMA((per_device,)),
            VMEM((mesh_rows, features), BF16),
            VMEM((mesh_rows, 2 * features), BF16),
            VMEM((mesh_rows, features), BF16),
            VMEM((mesh_rows, features), BF16),
            *weights_held(5 * tiles, features),
        ],
        "process",
        flops=6_000_000_000,
    )
    replies = exchange(answers, capacity, features).reshape(slots, features)
    (update,) = call(
        functools.partial(unpack_kernel, devices, per_device, capacity),
        [(ANY, replies), (HBM, decode_row), (HBM, decode_out)],
        [((grid_count, features), BF16)],
        [*held_like(decode_row, replies), VMEM((grid_count, features), BF16), *weights_held(tiles, features)],
        "unpack",
        flops=1_000_000_000,
    )
    return update


def solution(mesh):
    in_specs = (P(AXES, None), P(AXES, None), P(AXES), P(AXES), P(AXES), *[P()] * 13)
    return jax.shard_map(
        on_device, mesh=mesh, in_specs=in_specs, out_specs=P(AXES, None), check_vma=False
    )
```

```python
import functools

import jax
import jax.numpy as jnp
from jax import lax
from jax.experimental import pallas as pl
from jax.experimental.pallas import tpu as pltpu
from jax.sharding import PartitionSpec as P

HEADS = 16
BLOCK = 128
TILE = 512
LANES = 128
MASKED = -1e30
VMEM_MIB = 56
ENCODE_UNROLL = 4
PROCESS_UNROLL = 8
DECODE_UNROLL = 8
ANY, HBM, VMEM, SMEM = pl.ANY, pltpu.HBM, pltpu.VMEM, pltpu.SMEM
AXES = ("gx", "gy")
F32 = jnp.float32
BF16 = jnp.bfloat16
MIB = 1024 * 1024


def iota(shape, dim):
    return lax.broadcasted_iota(jnp.int32, shape, dim)


def floor_div(values, by):
    return jnp.floor((values.astype(F32) + 0.5) * (1.0 / by)).astype(jnp.int32)


def dot(left, right):
    return jnp.dot(left, right, preferred_element_type=F32)


def dot_t(left, right):
    return lax.dot_general(left, right, (((1,), (1,)), ((), ())), preferred_element_type=F32)


def dot_tl(left, right):
    return lax.dot_general(left, right, (((0,), (0,)), ((), ())), preferred_element_type=F32)


def normed(values, gain):
    wide = values.astype(F32)
    return wide * lax.rsqrt(jnp.mean(wide * wide, axis=-1, keepdims=True) + 1e-06) * gain


def block_hits(blocks, total_blocks):
    hits = iota((total_blocks, blocks.shape[1]), 0) == blocks
    return jnp.where(hits, 1.0, 0.0).astype(F32)


def block_counts(hits):
    counts = jnp.sum(hits, axis=1, keepdims=True)
    return jnp.broadcast_to(counts, (hits.shape[0], LANES)).astype(BF16)


def slots_of(hits, per_device, capacity):
    total_blocks, points = hits.shape
    earlier = jnp.where(iota((points, points), 0) < iota((points, points), 1), 1.0, 0.0)
    before = dot(hits.astype(BF16), earlier.astype(BF16))
    row, column = iota((total_blocks, total_blocks), 0), iota((total_blocks, total_blocks), 1)
    mates = (floor_div(row, per_device) == floor_div(column, per_device)) & (column < row)
    offset = dot(jnp.where(mates, 1.0, 0.0).astype(BF16), block_counts(hits))[:, :1]
    owner = floor_div(iota((total_blocks, 1), 0), per_device)
    base = owner.astype(F32) * capacity + offset
    return jnp.sum(hits * (base + before), axis=0, keepdims=True).astype(jnp.int32)


def placement(slot, slots):
    return jnp.where(iota((slots, slot.shape[1]), 0) == slot, 1.0, 0.0).astype(BF16)


class Fetch:
    def __init__(self, source, held, ready):
        self.copy = pltpu.make_async_copy(source, held, ready)
        self.held = held
        self.waiting = True
        self.copy.start()

    def __call__(self):
        if self.waiting:
            self.copy.wait()
            self.waiting = False
        return self.held


class Weight:
    def __init__(self, source, held, ready, base, count, first=0, semaphore=None):
        semaphore = base if semaphore is None else semaphore
        self.source, self.held, self.ready, self.base, self.count = source, held, ready, base, count
        self.semaphore = semaphore

        @pl.loop(0, count)
        def _(i):
            columns = pl.ds(pl.multiple_of((first + i) * TILE, TILE), TILE)
            pltpu.make_async_copy(source.at[:, columns], held.at[base + i], ready.at[semaphore + i]).start()

    def arrive(self, i):
        held = self.held.at[self.base + i]
        pltpu.make_async_copy(self.source.at[:, pl.ds(0, TILE)], held, self.ready.at[self.semaphore + i]).wait()
        return held

    def wait(self):
        @pl.loop(0, self.count)
        def _(i):
            self.arrive(i)

    def product(self, rows, put):
        @pl.loop(0, self.count)
        def _(i):
            held = self.arrive(i)
            put(pl.ds(pl.multiple_of(i * TILE, TILE), TILE), dot(rows[...], held[...]))


def product(rows, held, put):
    @pl.loop(0, held.shape[0])
    def _(i):
        put(pl.ds(pl.multiple_of(i * TILE, TILE), TILE), dot(rows[...], held[i]))


def store_in(ref):
    def put(columns, values):
        ref[:, columns] = values.astype(ref.dtype)

    return put


def count_lanes(encode_counts, decode_counts, devices, per_device):
    total_blocks = encode_counts.shape[0]
    lane = iota((devices, LANES), 1)
    labels = jnp.zeros((devices, LANES), F32)
    for kind, counts in enumerate((encode_counts, decode_counts)):
        for block in range(per_device):
            wanted = iota((devices, total_blocks), 0) * per_device + block
            wanted = jnp.where(iota((devices, total_blocks), 1) == wanted, 1.0, 0.0).astype(BF16)
            labels = labels + jnp.where(lane == kind * per_device + block, dot(wanted, counts), 0.0)
    return labels.astype(BF16)


def by_tiles(capacity):
    return capacity % 16 == 0


def fill_kernel(
    devices, per_device, capacity,
    state_hbm, encode_hbm, decode_hbm, gain_hbm, packed_ref,
    state_held, encode_held, decode_held, gain_held, ready,
):
    encode = Fetch(encode_hbm, encode_held, ready.at[0])
    decode = Fetch(decode_hbm, decode_held, ready.at[1])
    state = Fetch(state_hbm, state_held, ready.at[2])
    gain = Fetch(gain_hbm, gain_held, ready.at[3])
    total_blocks, slots = devices * per_device, devices * capacity
    encode_hits = block_hits(encode()[...], total_blocks)
    place = placement(slots_of(encode_hits, per_device, capacity), slots)
    decode_hits = block_hits(decode()[...], total_blocks)
    labels = count_lanes(block_counts(encode_hits), block_counts(decode_hits), devices, per_device)
    norm = normed(state()[...], gain()[...]).astype(BF16)
    features = norm.shape[1]
    if by_tiles(capacity):
        for tile in range(features // LANES):
            columns = dot(place, norm[:, tile * LANES : (tile + 1) * LANES]).astype(BF16)
            packed_ref[:, pl.ds(tile * capacity, capacity), :] = columns.reshape(devices, capacity, LANES)
        last = pl.ds(features // LANES * capacity, 8)
        packed_ref[:, last, :] = jnp.broadcast_to(labels[:, None, :], (devices, 8, LANES))
    else:
        packed_ref[:, pl.ds(0, features)] = dot(place, norm).astype(BF16)
        owner = floor_div(iota((slots, devices), 0), capacity) == iota((slots, devices), 1)
        packed_ref[:, pl.ds(features, LANES)] = dot(jnp.where(owner, 1.0, 0.0).astype(BF16), labels).astype(BF16)


def query_kernel(
    devices, per_device, capacity, scale,
    mesh_hbm, mesh_gain_hbm, encode_w, grid_hbm, grid_gain_hbm, decode_w, decode_hbm,
    query_ref, packed_ref,
    mesh_held, mesh_gain_held, grid_held, grid_gain_held, decode_held, ready,
    norm_ref, weights, arrived,
):
    decode = Fetch(decode_hbm, decode_held, ready.at[0])
    grid = Fetch(grid_hbm, grid_held, ready.at[1])
    grid_gain = Fetch(grid_gain_hbm, grid_gain_held, ready.at[2])
    mesh = Fetch(mesh_hbm, mesh_held, ready.at[3])
    mesh_gain = Fetch(mesh_gain_hbm, mesh_gain_held, ready.at[4])
    count = encode_w.shape[1] // TILE
    decode_weight = Weight(decode_w, weights, arrived, 0, count)
    encode_weight = Weight(encode_w, weights, arrived, count, count)
    slots = packed_ref.shape[0]
    hits = block_hits(decode()[...], devices * per_device)
    place = placement(slots_of(hits, per_device, capacity), slots)
    norm_ref[...] = normed(grid()[...], grid_gain()[...]).astype(BF16)

    def put_packed(columns, values):
        rounded = (values.astype(BF16).astype(F32) * scale).astype(BF16)
        packed_ref[:, columns] = dot(place, rounded).astype(BF16)

    decode_weight.product(norm_ref, put_packed)
    norm_ref[...] = normed(mesh()[...], mesh_gain()[...]).astype(BF16)

    def put_query(columns, values):
        query_ref[:, columns] = (values.astype(BF16).astype(F32) * scale).astype(BF16)

    encode_weight.product(norm_ref, put_query)


def lanes_of(labels, first, count):
    row, lane = iota((8, LANES), 0), iota((8, LANES), 1)
    wanted = (lane == row + first) & (row < count)
    return dot_t(jnp.where(wanted, 1.0, 0.0).astype(BF16), labels).astype(BF16)


def even_lanes(shape, head_size):
    return iota(shape, len(shape) - 1) < head_size


def split_heads(values, head_size):
    even = even_lanes(values.shape, head_size)
    zero = jnp.zeros_like(values)
    return jnp.concatenate([jnp.where(even, values, zero), jnp.where(even, zero, values)], axis=0)


def join_heads(values, head_size):
    rows = values.shape[0] // 2
    even = even_lanes((rows, values.shape[1]), head_size)
    return jnp.where(even, values[:rows], values[rows:])


def encode_kernel(
    per_device, capacity, head_size, unroll,
    received_hbm, query_hbm, mesh_hbm, gain_hbm, keyval_w, out_w,
    mid_ref, norm_ref, labels_ref,
    received_held, query_held, mesh_held, gain_held, ready,
    rows_ref, keyval, attended, bias, weights, arrived,
):
    features = mid_ref.shape[1]
    devices = labels_ref.shape[0]
    slots = devices * capacity
    kv_count, out_count = keyval_w.shape[1] // TILE, features // TILE
    received = Fetch(received_hbm, received_held, ready.at[0])
    keyval_weight = Weight(keyval_w, weights, arrived, 0, kv_count)
    query_rows = Fetch(query_hbm, query_held, ready.at[1])
    out_weight = Weight(out_w, weights, arrived, kv_count, out_count)
    mesh = Fetch(mesh_hbm, mesh_held, ready.at[2])
    gain = Fetch(gain_hbm, gain_held, ready.at[3])
    received_ref = received()
    if by_tiles(capacity):
        for tile in range(features // LANES):
            part = received_ref[:, pl.ds(tile * capacity, capacity), :]
            rows_ref[:, pl.ds(tile * LANES, LANES)] = part.reshape(slots, LANES)
        last = received_ref[:, pl.ds(features // LANES * capacity, 8), :]
        labels = jnp.max(last.astype(F32), axis=1).astype(BF16)
        rows = rows_ref
    else:
        rows = received_ref.at[:, pl.ds(0, features)]
        first = iota((devices, slots), 1) == iota((devices, slots), 0) * capacity
        labels = dot(jnp.where(first, 1.0, 0.0).astype(BF16), received_ref[:, pl.ds(features, LANES)]).astype(BF16)
    labels_ref[...] = labels
    keyval_weight.product(rows, store_in(keyval))

    sender = floor_div(iota((devices, slots), 1), capacity) == iota((devices, slots), 0)
    filled = dot(lanes_of(labels, 0, per_device), jnp.where(sender, 1.0, 0.0).astype(BF16))
    lane = iota((1, slots), 1)
    place = (lane - floor_div(lane, capacity) * capacity).astype(F32)
    begin = jnp.zeros((1, slots), F32)
    for block in range(per_device):
        end = begin + filled[block : block + 1]
        bias[block : block + 1] = jnp.where((place >= begin) & (place < end), 0.0, MASKED)
        begin = end
    query_ref = query_rows()

    @pl.loop(0, features // LANES, unroll=unroll)
    def _(pair):
        columns = pl.ds(pl.multiple_of(pair * LANES, LANES), LANES)
        value_columns = pl.ds(pl.multiple_of(features + pair * LANES, LANES), LANES)
        keys, values = keyval[:, columns], keyval[:, value_columns]
        for block in range(per_device):
            block_rows = pl.ds(block * BLOCK, BLOCK)
            queries = split_heads(query_ref[block_rows, columns], head_size)
            scores = dot_t(queries, keys) + bias[block : block + 1]
            powers = jnp.exp(scores - jnp.max(scores, axis=-1, keepdims=True))
            sums = jnp.sum(powers, axis=-1, keepdims=True)
            output = dot(powers.astype(BF16), values) / sums
            attended[block_rows, columns] = join_heads(output, head_size).astype(BF16)

    mesh_ref = mesh()

    def put_mid(columns, values):
        mid_ref[:, columns] = (mesh_ref[:, columns].astype(F32) + values).astype(BF16)

    out_weight.product(attended, put_mid)
    norm_ref[...] = normed(mid_ref[...], gain()[...]).astype(BF16)


def own_kernel(scale, norm_hbm, qkv_w, qkv_ref, norm_held, ready, qkv_held, arrived):
    features = norm_hbm.shape[1]
    norm = Fetch(norm_hbm, norm_held, ready.at[0])
    weight = Weight(qkv_w, qkv_held, arrived, 0, qkv_held.shape[0])
    weight.product(norm(), store_in(qkv_ref))
    queries = pl.ds(0, features)
    qkv_ref[:, queries] = (qkv_ref[:, queries].astype(F32) * scale).astype(BF16)


def hold_kernel(
    qkv_w, out_w, decode_w, qkv_hbm, mid_hbm, queries_hbm,
    kv_kept, out_kept, decode_kept, qkv_kept, mid_kept, queries_kept,
    ready, arrived,
):
    tiles = out_kept.shape[0]
    weights = [
        Weight(qkv_w, kv_kept, arrived, 0, 2 * tiles, tiles),
        Weight(out_w, out_kept, arrived, 0, tiles, 0, 2 * tiles),
        Weight(decode_w, decode_kept, arrived, 0, 2 * tiles, 0, 3 * tiles),
    ]
    rows = [
        Fetch(source, kept, ready.at[i])
        for i, (source, kept) in enumerate(((qkv_hbm, qkv_kept), (mid_hbm, mid_kept), (queries_hbm, queries_kept)))
    ]
    for weight in weights:
        weight.wait()
    for row in rows:
        row()


def process_kernel(
    per_device, capacity, head_size, unroll, decode_unroll,
    me_ref, neighbour_ref, first_hbm, norm_hbm, second_hbm, qkv_ref, mid_ref, gain_hbm, queries_ref, labels_hbm,
    kv_w, out_w, decode_w,
    answers_ref,
    gain_held, labels_held, ready, picked,
    chosen, other, attended, mesh_out,
):
    features = mid_ref.shape[1]
    odd = me_ref[0] % 2
    for block in range(per_device):
        rows = pl.ds(block * BLOCK, BLOCK)
        position = neighbour_ref[block] - me_ref[0] * per_device + per_device
        sides = ((first_hbm, 2 * (1 - odd)), (norm_hbm, 1), (second_hbm, 2 * odd))
        for source, side in sides:
            for place in range(per_device):
                @pl.when(position == side * per_device + place)
                def _():
                    block_rows = source.at[pl.ds(place * BLOCK, BLOCK)]
                    pltpu.make_async_copy(block_rows, chosen.at[rows], picked.at[block]).start()

    gain = Fetch(gain_hbm, gain_held, ready.at[0])
    labels = Fetch(labels_hbm, labels_held, ready.at[1])
    for block in range(per_device):
        rows = pl.ds(block * BLOCK, BLOCK)
        pltpu.make_async_copy(norm_hbm.at[rows], chosen.at[rows], picked.at[block]).wait()
    product(chosen, kv_w, store_in(other))

    @pl.loop(0, features // LANES, unroll=unroll)
    def _(pair):
        columns = pl.ds(pl.multiple_of(pair * LANES, LANES), LANES)
        second = pl.ds(pl.multiple_of(features + pair * LANES, LANES), LANES)
        third = pl.ds(pl.multiple_of(2 * features + pair * LANES, LANES), LANES)
        for block in range(per_device):
            rows = pl.ds(block * BLOCK, BLOCK)
            queries = split_heads(qkv_ref[rows, columns], head_size)
            keys = jnp.concatenate([qkv_ref[rows, second], other[rows, columns]], axis=0)
            values = jnp.concatenate([qkv_ref[rows, third], other[rows, second]], axis=0)
            scores = dot_t(queries, keys)
            powers = jnp.exp(scores - jnp.max(scores, axis=-1, keepdims=True))
            sums = jnp.sum(powers, axis=-1, keepdims=True)
            output = dot(powers.astype(BF16), values) / sums
            attended[rows, columns] = join_heads(output, head_size).astype(BF16)

    def put_out(columns, values):
        mesh_out[:, columns] = (mid_ref[:, columns].astype(F32) + values).astype(BF16)

    product(attended, out_w, put_out)
    chosen[...] = normed(mesh_out[...], gain()[...]).astype(BF16)
    product(chosen, decode_w, store_in(other))
    decode_points(
        per_device, capacity, head_size, decode_unroll, other, queries_ref, labels()[...], answers_ref
    )


def decode_points(per_device, capacity, head_size, unroll, other, queries_ref, labels, answers_ref):
    slots, features = answers_ref.shape
    devices = labels.shape[0]
    sender = floor_div(iota((slots, devices), 0), capacity) == iota((slots, devices), 1)
    filled = dot_t(jnp.where(sender, 1.0, 0.0).astype(BF16), lanes_of(labels, per_device, per_device))
    row = iota((slots, 1), 0)
    place = (row - floor_div(row, capacity) * capacity).astype(F32)
    reads, begin = [], jnp.zeros((slots, 1), F32)
    for block in range(per_device):
        end = begin + filled[:, block : block + 1]
        here = jnp.where((place >= begin) & (place < end), 1.0, 0.0)
        reads.append(jnp.broadcast_to(here, (slots, BLOCK)))
        begin = end

    @pl.loop(0, features // LANES, unroll=unroll)
    def _(pair):
        columns = pl.ds(pl.multiple_of(pair * LANES, LANES), LANES)
        second = pl.ds(pl.multiple_of(features + pair * LANES, LANES), LANES)
        queries = queries_ref[:, columns]
        even = even_lanes((slots, LANES), head_size)
        outputs = []
        for head in range(LANES // head_size):
            picked = jnp.where(even if head == 0 else ~even, queries, jnp.zeros_like(queries))
            scores = dot_t(picked, other[:, columns])
            chosen_scores = scores[:, :BLOCK]
            for block in range(1, per_device):
                here = scores[:, block * BLOCK : (block + 1) * BLOCK]
                chosen_scores = jnp.where(reads[block] > 0.5, here, chosen_scores)
            powers = jnp.exp(chosen_scores - jnp.max(chosen_scores, axis=-1, keepdims=True))
            sums = jnp.sum(powers, axis=-1, keepdims=True)
            spread = jnp.concatenate(
                [jnp.where(reads[block] > 0.5, powers, 0.0).astype(BF16) for block in range(per_device)], axis=1
            )
            outputs.append(dot(spread, other[:, second]) / sums)
        answers_ref[:, columns] = jnp.where(even, outputs[0], outputs[1]).astype(BF16)


def unpack_kernel(
    devices, per_device, capacity, replies_hbm, decode_hbm, out_w, update_ref,
    decode_held, replies_held, ready, decoded, weights, arrived,
):
    decode = Fetch(decode_hbm, decode_held, ready.at[0])
    replies = Fetch(replies_hbm, replies_held, ready.at[1])
    weight = Weight(out_w, weights, arrived, 0, out_w.shape[1] // TILE)
    hits = block_hits(decode()[...], devices * per_device)
    place = placement(slots_of(hits, per_device, capacity), replies_hbm.shape[0])
    decoded[...] = dot_tl(place, replies()[...]).astype(BF16)
    weight.product(decoded, store_in(update_ref))


def call(kernel, operands, outs, scratch, name, flops, limit=VMEM_MIB):
    return pl.pallas_call(
        kernel,
        out_shape=[jax.ShapeDtypeStruct(*out) if isinstance(out, tuple) else out for out in outs],
        in_specs=[pl.BlockSpec(memory_space=space) for space, _ in operands],
        out_specs=[pl.BlockSpec(memory_space=VMEM) for _ in outs],
        scratch_shapes=scratch,
        name=name,
        cost_estimate=pl.CostEstimate(flops=flops, bytes_accessed=4 * MIB, transcendentals=0),
        compiler_params=pltpu.CompilerParams(vmem_limit_bytes=limit * MIB),
    )(*[pltpu.with_memory_space_constraint(value, HBM) if space is HBM else value for space, value in operands])


def held_like(*values):
    return [*[VMEM(value.shape, value.dtype) for value in values], pltpu.SemaphoreType.DMA((len(values),))]


def weights_held(count, features):
    return [VMEM((count, features, TILE), BF16), pltpu.SemaphoreType.DMA((count,))]


def on_device(
    grid_state,
    mesh_state,
    encode_block,
    neighbour_block,
    decode_block,
    encode_grid_gain,
    encode_mesh_gain,
    process_gain,
    decode_grid_gain,
    decode_mesh_gain,
    encode_query,
    encode_keyval,
    encode_out,
    process_qkv,
    process_out,
    decode_query,
    decode_keyval,
    decode_out,
):
    devices = lax.axis_size(AXES)
    me = lax.axis_index(AXES)
    grid_count, features = grid_state.shape
    mesh_rows = mesh_state.shape[0]
    per_device = mesh_rows // BLOCK
    total_blocks = per_device * devices
    capacity = max(4, 2 * grid_count // devices)
    slots = devices * capacity
    head_size = features // HEADS
    scale = head_size ** (-0.5)
    tiles = features // TILE
    me_row = me.astype(jnp.int32).reshape(1)
    encode_row, decode_row = encode_block.reshape(1, -1), decode_block.reshape(1, -1)
    encode_grid_gain, encode_mesh_gain, process_gain, decode_grid_gain, decode_mesh_gain = [
        gain.reshape(1, -1)
        for gain in (encode_grid_gain, encode_mesh_gain, process_gain, decode_grid_gain, decode_mesh_gain)
    ]

    def exchange(rows, *shape):
        return lax.all_to_all(rows.reshape(devices, *shape), AXES, split_axis=0, concat_axis=0, tiled=True)

    if by_tiles(capacity):
        payload = (capacity * features // LANES + 8, LANES)
        packed_shape = (devices, *payload)
    else:
        payload = (capacity, features + LANES)
        packed_shape = (slots, features + LANES)
    (packed,) = call(
        functools.partial(fill_kernel, devices, per_device, capacity),
        [(HBM, grid_state), (HBM, encode_row), (HBM, decode_row), (HBM, encode_grid_gain)],
        [(packed_shape, BF16)],
        held_like(grid_state, encode_row, decode_row, encode_grid_gain),
        "fill",
        flops=600_000_000,
    )
    received = exchange(packed, *payload).reshape(packed_shape)
    query, packed_queries = call(
        functools.partial(query_kernel, devices, per_device, capacity, scale),
        [
            (HBM, mesh_state), (HBM, encode_mesh_gain), (HBM, encode_query),
            (HBM, grid_state), (HBM, decode_grid_gain), (HBM, decode_query), (HBM, decode_row),
        ],
        [((mesh_rows, features), BF16), ((slots, features), BF16)],
        [
            *held_like(mesh_state, encode_mesh_gain, grid_state, decode_grid_gain, decode_row),
            VMEM((grid_count, features), BF16),
            *weights_held(2 * tiles, features),
        ],
        "queries",
        flops=2_000_000_000,
    )
    arrived_queries = exchange(packed_queries, capacity, features).reshape(slots, features)
    mesh_mid, process_norm, labels = call(
        functools.partial(encode_kernel, per_device, capacity, head_size, ENCODE_UNROLL),
        [
            (ANY, received), (HBM, query), (HBM, mesh_state), (HBM, process_gain),
            (HBM, encode_keyval), (HBM, encode_out),
        ],
        [((mesh_rows, features), BF16), ((mesh_rows, features), BF16), ((devices, LANES), BF16)],
        [
            *held_like(received, query, mesh_state, process_gain),
            VMEM((slots, features), BF16),
            VMEM((slots, 2 * features), BF16),
            VMEM((mesh_rows, features), BF16),
            VMEM((8, slots), F32),
            *weights_held(3 * tiles, features),
        ],
        "encode",
        flops=5_000_000_000,
    )
    pairs = [(i, i ^ 1) for i in range(devices)]
    across = [(i, i + 1 if i % 2 else i - 1) for i in range(1, devices - 1)]
    first = lax.ppermute(process_norm, AXES, pairs)
    second = lax.ppermute(process_norm, AXES, across)
    (mesh_qkv,) = call(
        functools.partial(own_kernel, scale),
        [(HBM, process_norm), (HBM, process_qkv)],
        [((mesh_rows, 3 * features), BF16)],
        [
            *held_like(process_norm),
            VMEM((3 * tiles, features, TILE), BF16),
            pltpu.SemaphoreType.DMA((3 * tiles,)),
        ],
        "own",
        flops=2_000_000_000,
    )
    kv_w, out_w, decode_w, mesh_qkv, mesh_mid, arrived_queries = call(
        hold_kernel,
        [
            (HBM, process_qkv), (HBM, process_out), (HBM, decode_keyval),
            (HBM, mesh_qkv), (HBM, mesh_mid), (ANY, arrived_queries),
        ],
        [
            *[VMEM((count * tiles, features, TILE), BF16) for count in (2, 1, 2)],
            *[VMEM(rows.shape, BF16) for rows in (mesh_qkv, mesh_mid, arrived_queries)],
        ],
        [pltpu.SemaphoreType.DMA((3,)), pltpu.SemaphoreType.DMA((5 * tiles,))],
        "hold",
        flops=2_000_000_000,
        limit=36,
    )
    (answers,) = call(
        functools.partial(process_kernel, per_device, capacity, head_size, PROCESS_UNROLL, DECODE_UNROLL),
        [
            (SMEM, me_row), (SMEM, neighbour_block), (ANY, first), (ANY, process_norm), (ANY, second),
            (VMEM, mesh_qkv), (VMEM, mesh_mid), (HBM, decode_mesh_gain), (VMEM, arrived_queries), (HBM, labels),
            (VMEM, kv_w), (VMEM, out_w), (VMEM, decode_w),
        ],
        [((slots, features), BF16)],
        [
            *held_like(decode_mesh_gain, labels),
            pltpu.SemaphoreType.DMA((per_device,)),
            VMEM((mesh_rows, features), BF16),
            VMEM((mesh_rows, 2 * features), BF16),
            VMEM((mesh_rows, features), BF16),
            VMEM((mesh_rows, features), BF16),
        ],
        "process",
        flops=8_000_000_000,
        limit=36,
    )
    replies = exchange(answers, capacity, features).reshape(slots, features)
    (update,) = call(
        functools.partial(unpack_kernel, devices, per_device, capacity),
        [(ANY, replies), (HBM, decode_row), (HBM, decode_out)],
        [((grid_count, features), BF16)],
        [*held_like(decode_row, replies), VMEM((grid_count, features), BF16), *weights_held(tiles, features)],
        "unpack",
        flops=1_000_000_000,
    )
    return update


def solution(mesh):
    in_specs = (P(AXES, None), P(AXES, None), P(AXES), P(AXES), P(AXES), *[P()] * 13)
    return jax.shard_map(
        on_device, mesh=mesh, in_specs=in_specs, out_specs=P(AXES, None), check_vma=False
    )
```

```python
import functools

import jax
import jax.numpy as jnp
from jax import lax
from jax.experimental import pallas as pl
from jax.experimental.pallas import tpu as pltpu
from jax.sharding import PartitionSpec as P

HEADS = 16
BLOCK = 128
TILE = 512
LANES = 128
MASKED = -1e30
VMEM_MIB = 56
ENCODE_UNROLL = 4
PROCESS_UNROLL = 8
DECODE_UNROLL = 8
ANY, HBM, VMEM, SMEM = pl.ANY, pltpu.HBM, pltpu.VMEM, pltpu.SMEM
AXES = ("gx", "gy")
F32 = jnp.float32
BF16 = jnp.bfloat16
MIB = 1024 * 1024


def iota(shape, dim):
    return lax.broadcasted_iota(jnp.int32, shape, dim)


def floor_div(values, by):
    return jnp.floor((values.astype(F32) + 0.5) * (1.0 / by)).astype(jnp.int32)


def dot(left, right):
    return jnp.dot(left, right, preferred_element_type=F32)


def dot_t(left, right):
    return lax.dot_general(left, right, (((1,), (1,)), ((), ())), preferred_element_type=F32)


def dot_tl(left, right):
    return lax.dot_general(left, right, (((0,), (0,)), ((), ())), preferred_element_type=F32)


def normed(values, gain):
    wide = values.astype(F32)
    return wide * lax.rsqrt(jnp.mean(wide * wide, axis=-1, keepdims=True) + 1e-06) * gain


def block_hits(blocks, total_blocks):
    hits = iota((total_blocks, blocks.shape[1]), 0) == blocks
    return jnp.where(hits, 1.0, 0.0).astype(F32)


def block_counts(hits):
    counts = jnp.sum(hits, axis=1, keepdims=True)
    return jnp.broadcast_to(counts, (hits.shape[0], LANES)).astype(BF16)


def slots_of(hits, per_device, capacity):
    total_blocks, points = hits.shape
    earlier = jnp.where(iota((points, points), 0) < iota((points, points), 1), 1.0, 0.0)
    before = dot(hits.astype(BF16), earlier.astype(BF16))
    row, column = iota((total_blocks, total_blocks), 0), iota((total_blocks, total_blocks), 1)
    mates = (floor_div(row, per_device) == floor_div(column, per_device)) & (column < row)
    offset = dot(jnp.where(mates, 1.0, 0.0).astype(BF16), block_counts(hits))[:, :1]
    owner = floor_div(iota((total_blocks, 1), 0), per_device)
    base = owner.astype(F32) * capacity + offset
    return jnp.sum(hits * (base + before), axis=0, keepdims=True).astype(jnp.int32)


def placement(slot, slots):
    return jnp.where(iota((slots, slot.shape[1]), 0) == slot, 1.0, 0.0).astype(BF16)


class Fetch:
    def __init__(self, source, held, ready):
        self.copy = pltpu.make_async_copy(source, held, ready)
        self.held = held
        self.waiting = True
        self.copy.start()

    def __call__(self):
        if self.waiting:
            self.copy.wait()
            self.waiting = False
        return self.held


class Weight:
    def __init__(self, source, held, ready, base, count, first=0, semaphore=None):
        semaphore = base if semaphore is None else semaphore
        self.source, self.held, self.ready, self.base, self.count = source, held, ready, base, count
        self.semaphore = semaphore

        @pl.loop(0, count)
        def _(i):
            columns = pl.ds(pl.multiple_of((first + i) * TILE, TILE), TILE)
            pltpu.make_async_copy(source.at[:, columns], held.at[base + i], ready.at[semaphore + i]).start()

    def arrive(self, i):
        held = self.held.at[self.base + i]
        pltpu.make_async_copy(self.source.at[:, pl.ds(0, TILE)], held, self.ready.at[self.semaphore + i]).wait()
        return held

    def wait(self):
        @pl.loop(0, self.count)
        def _(i):
            self.arrive(i)

    def product(self, rows, put):
        for i in range(self.count):
            put(pl.ds(i * TILE, TILE), dot(rows[...], self.arrive(i)[...]))


def product(rows, held, put):
    for i in range(held.shape[0]):
        put(pl.ds(i * TILE, TILE), dot(rows[...], held[i]))


def store_in(ref):
    def put(columns, values):
        ref[:, columns] = values.astype(ref.dtype)

    return put


def count_lanes(encode_counts, decode_counts, devices, per_device):
    total_blocks = encode_counts.shape[0]
    lane = iota((devices, LANES), 1)
    labels = jnp.zeros((devices, LANES), F32)
    for kind, counts in enumerate((encode_counts, decode_counts)):
        for block in range(per_device):
            wanted = iota((devices, total_blocks), 0) * per_device + block
            wanted = jnp.where(iota((devices, total_blocks), 1) == wanted, 1.0, 0.0).astype(BF16)
            labels = labels + jnp.where(lane == kind * per_device + block, dot(wanted, counts), 0.0)
    return labels.astype(BF16)


def by_tiles(capacity):
    return capacity % 16 == 0


def fill_kernel(
    devices, per_device, capacity,
    state_hbm, encode_hbm, decode_hbm, gain_hbm, packed_hbm,
    state_held, encode_held, decode_held, gain_held, ready, packed_ref, sent,
):
    encode = Fetch(encode_hbm, encode_held, ready.at[0])
    decode = Fetch(decode_hbm, decode_held, ready.at[1])
    state = Fetch(state_hbm, state_held, ready.at[2])
    gain = Fetch(gain_hbm, gain_held, ready.at[3])
    total_blocks, slots = devices * per_device, devices * capacity
    encode_hits = block_hits(encode()[...], total_blocks)
    place = placement(slots_of(encode_hits, per_device, capacity), slots)
    decode_hits = block_hits(decode()[...], total_blocks)
    labels = count_lanes(block_counts(encode_hits), block_counts(decode_hits), devices, per_device)
    norm = normed(state()[...], gain()[...]).astype(BF16)
    features = norm.shape[1]
    copies = []

    def send(place):
        copies.append(pltpu.make_async_copy(packed_ref.at[place], packed_hbm.at[place], sent.at[len(copies)]))
        copies[-1].start()

    if by_tiles(capacity):
        last = (slice(None), pl.ds(features // LANES * capacity, 8))
        packed_ref[last] = jnp.broadcast_to(labels[:, None, :], (devices, 8, LANES))
        send(last)
        for tile in range(features // LANES):
            columns = dot(place, norm[:, tile * LANES : (tile + 1) * LANES]).astype(BF16)
            rows = (slice(None), pl.ds(tile * capacity, capacity))
            packed_ref[rows] = columns.reshape(devices, capacity, LANES)
            send(rows)
    else:
        packed_ref[:, pl.ds(0, features)] = dot(place, norm).astype(BF16)
        owner = floor_div(iota((slots, devices), 0), capacity) == iota((slots, devices), 1)
        packed_ref[:, pl.ds(features, LANES)] = dot(jnp.where(owner, 1.0, 0.0).astype(BF16), labels).astype(BF16)
        send((slice(None), slice(None)))
    for copy in copies:
        copy.wait()


def query_kernel(
    devices, per_device, capacity, scale,
    mesh_hbm, mesh_gain_hbm, encode_w, grid_hbm, grid_gain_hbm, decode_w, decode_hbm,
    query_ref, packed_ref, back_ref,
    mesh_held, mesh_gain_held, grid_held, grid_gain_held, decode_held, ready,
    norm_ref, weights, arrived,
):
    decode = Fetch(decode_hbm, decode_held, ready.at[0])
    grid = Fetch(grid_hbm, grid_held, ready.at[1])
    grid_gain = Fetch(grid_gain_hbm, grid_gain_held, ready.at[2])
    mesh = Fetch(mesh_hbm, mesh_held, ready.at[3])
    mesh_gain = Fetch(mesh_gain_hbm, mesh_gain_held, ready.at[4])
    count = encode_w.shape[1] // TILE
    decode_weight = Weight(decode_w, weights, arrived, 0, count)
    encode_weight = Weight(encode_w, weights, arrived, count, count)
    slots = packed_ref.shape[0]
    hits = block_hits(decode()[...], devices * per_device)
    place = placement(slots_of(hits, per_device, capacity), slots)
    back_ref[...] = place.T
    norm_ref[...] = normed(grid()[...], grid_gain()[...]).astype(BF16)

    def put_packed(columns, values):
        rounded = (values.astype(BF16).astype(F32) * scale).astype(BF16)
        packed_ref[:, columns] = dot(place, rounded).astype(BF16)

    decode_weight.product(norm_ref, put_packed)
    norm_ref[...] = normed(mesh()[...], mesh_gain()[...]).astype(BF16)

    def put_query(columns, values):
        query_ref[:, columns] = (values.astype(BF16).astype(F32) * scale).astype(BF16)

    encode_weight.product(norm_ref, put_query)


def lanes_of(labels, first, count):
    row, lane = iota((8, LANES), 0), iota((8, LANES), 1)
    wanted = (lane == row + first) & (row < count)
    return dot_t(jnp.where(wanted, 1.0, 0.0).astype(BF16), labels).astype(BF16)


def even_lanes(shape, head_size):
    return iota(shape, len(shape) - 1) < head_size


def split_heads(values, head_size):
    even = even_lanes(values.shape, head_size)
    zero = jnp.zeros_like(values)
    return jnp.concatenate([jnp.where(even, values, zero), jnp.where(even, zero, values)], axis=0)


def join_heads(values, head_size):
    rows = values.shape[0] // 2
    even = even_lanes((rows, values.shape[1]), head_size)
    return jnp.where(even, values[:rows], values[rows:])


def encode_kernel(
    per_device, capacity, head_size, unroll,
    received_hbm, query_hbm, mesh_hbm, gain_hbm, keyval_w, out_w,
    mid_ref, norm_ref, labels_ref,
    received_held, query_held, mesh_held, gain_held, ready,
    rows_ref, keyval, attended, bias, weights, arrived,
):
    features = mid_ref.shape[1]
    devices = labels_ref.shape[0]
    slots = devices * capacity
    kv_count, out_count = keyval_w.shape[1] // TILE, features // TILE
    received = Fetch(received_hbm, received_held, ready.at[0])
    keyval_weight = Weight(keyval_w, weights, arrived, 0, kv_count)
    query_rows = Fetch(query_hbm, query_held, ready.at[1])
    out_weight = Weight(out_w, weights, arrived, kv_count, out_count)
    mesh = Fetch(mesh_hbm, mesh_held, ready.at[2])
    gain = Fetch(gain_hbm, gain_held, ready.at[3])
    received_ref = received()
    if by_tiles(capacity):
        for tile in range(features // LANES):
            part = received_ref[:, pl.ds(tile * capacity, capacity), :]
            rows_ref[:, pl.ds(tile * LANES, LANES)] = part.reshape(slots, LANES)
        last = received_ref[:, pl.ds(features // LANES * capacity, 8), :]
        labels = jnp.max(last.astype(F32), axis=1).astype(BF16)
        rows = rows_ref
    else:
        rows = received_ref.at[:, pl.ds(0, features)]
        first = iota((devices, slots), 1) == iota((devices, slots), 0) * capacity
        labels = dot(jnp.where(first, 1.0, 0.0).astype(BF16), received_ref[:, pl.ds(features, LANES)]).astype(BF16)
    labels_ref[...] = labels
    keyval_weight.product(rows, store_in(keyval))

    sender = floor_div(iota((devices, slots), 1), capacity) == iota((devices, slots), 0)
    filled = dot(lanes_of(labels, 0, per_device), jnp.where(sender, 1.0, 0.0).astype(BF16))
    lane = iota((1, slots), 1)
    place = (lane - floor_div(lane, capacity) * capacity).astype(F32)
    begin = jnp.zeros((1, slots), F32)
    for block in range(per_device):
        end = begin + filled[block : block + 1]
        bias[block : block + 1] = jnp.where((place >= begin) & (place < end), 0.0, MASKED)
        begin = end
    query_ref = query_rows()

    @pl.loop(0, features // LANES, unroll=unroll)
    def _(pair):
        columns = pl.ds(pl.multiple_of(pair * LANES, LANES), LANES)
        value_columns = pl.ds(pl.multiple_of(features + pair * LANES, LANES), LANES)
        keys, values = keyval[:, columns], keyval[:, value_columns]
        for block in range(per_device):
            block_rows = pl.ds(block * BLOCK, BLOCK)
            queries = split_heads(query_ref[block_rows, columns], head_size)
            scores = dot_t(queries, keys) + bias[block : block + 1]
            powers = jnp.exp(scores - jnp.max(scores, axis=-1, keepdims=True))
            sums = jnp.sum(powers, axis=-1, keepdims=True)
            output = dot(powers.astype(BF16), values) / sums
            attended[block_rows, columns] = join_heads(output, head_size).astype(BF16)

    mesh_ref = mesh()

    def put_mid(columns, values):
        mid_ref[:, columns] = (mesh_ref[:, columns].astype(F32) + values).astype(BF16)

    out_weight.product(attended, put_mid)
    norm_ref[...] = normed(mid_ref[...], gain()[...]).astype(BF16)


def own_kernel(scale, norm_hbm, qkv_w, qkv_ref, norm_held, ready, qkv_held, arrived):
    features = norm_hbm.shape[1]
    norm = Fetch(norm_hbm, norm_held, ready.at[0])
    weight = Weight(qkv_w, qkv_held, arrived, 0, qkv_held.shape[0])
    weight.product(norm(), store_in(qkv_ref))
    queries = pl.ds(0, features)
    qkv_ref[:, queries] = (qkv_ref[:, queries].astype(F32) * scale).astype(BF16)


def hold_kernel(
    qkv_w, out_w, decode_w, qkv_hbm, mid_hbm, queries_hbm,
    kv_kept, out_kept, decode_kept, qkv_kept, mid_kept, queries_kept,
    ready, arrived,
):
    tiles = out_kept.shape[0]
    weights = [
        Weight(qkv_w, kv_kept, arrived, 0, 2 * tiles, tiles),
        Weight(out_w, out_kept, arrived, 0, tiles, 0, 2 * tiles),
        Weight(decode_w, decode_kept, arrived, 0, 2 * tiles, 0, 3 * tiles),
    ]
    rows = [
        Fetch(source, kept, ready.at[i])
        for i, (source, kept) in enumerate(((qkv_hbm, qkv_kept), (mid_hbm, mid_kept), (queries_hbm, queries_kept)))
    ]
    for weight in weights:
        weight.wait()
    for row in rows:
        row()


def process_kernel(
    per_device, capacity, head_size, unroll, decode_unroll,
    me_ref, neighbour_ref, first_hbm, norm_hbm, second_hbm, qkv_ref, mid_ref, gain_hbm, queries_ref, labels_hbm,
    kv_w, out_w, decode_w,
    answers_ref,
    gain_held, labels_held, ready, picked,
    chosen, other, attended, mesh_out,
):
    features = mid_ref.shape[1]
    odd = me_ref[0] % 2
    for block in range(per_device):
        rows = pl.ds(block * BLOCK, BLOCK)
        position = neighbour_ref[block] - me_ref[0] * per_device + per_device
        sides = ((first_hbm, 2 * (1 - odd)), (norm_hbm, 1), (second_hbm, 2 * odd))
        for source, side in sides:
            for place in range(per_device):
                @pl.when(position == side * per_device + place)
                def _():
                    block_rows = source.at[pl.ds(place * BLOCK, BLOCK)]
                    pltpu.make_async_copy(block_rows, chosen.at[rows], picked.at[block]).start()

    gain = Fetch(gain_hbm, gain_held, ready.at[0])
    labels = Fetch(labels_hbm, labels_held, ready.at[1])
    for block in range(per_device):
        rows = pl.ds(block * BLOCK, BLOCK)
        pltpu.make_async_copy(norm_hbm.at[rows], chosen.at[rows], picked.at[block]).wait()
    product(chosen, kv_w, store_in(other))

    @pl.loop(0, features // LANES, unroll=unroll)
    def _(pair):
        columns = pl.ds(pl.multiple_of(pair * LANES, LANES), LANES)
        second = pl.ds(pl.multiple_of(features + pair * LANES, LANES), LANES)
        third = pl.ds(pl.multiple_of(2 * features + pair * LANES, LANES), LANES)
        for block in range(per_device):
            rows = pl.ds(block * BLOCK, BLOCK)
            queries = split_heads(qkv_ref[rows, columns], head_size)
            keys = jnp.concatenate([qkv_ref[rows, second], other[rows, columns]], axis=0)
            values = jnp.concatenate([qkv_ref[rows, third], other[rows, second]], axis=0)
            scores = dot_t(queries, keys)
            powers = jnp.exp(scores - jnp.max(scores, axis=-1, keepdims=True))
            sums = jnp.sum(powers, axis=-1, keepdims=True)
            output = dot(powers.astype(BF16), values) / sums
            attended[rows, columns] = join_heads(output, head_size).astype(BF16)

    def put_out(columns, values):
        mesh_out[:, columns] = (mid_ref[:, columns].astype(F32) + values).astype(BF16)

    product(attended, out_w, put_out)
    chosen[...] = normed(mesh_out[...], gain()[...]).astype(BF16)
    product(chosen, decode_w, store_in(other))
    decode_points(
        per_device, capacity, head_size, decode_unroll, other, queries_ref, labels()[...], answers_ref
    )


def decode_points(per_device, capacity, head_size, unroll, other, queries_ref, labels, answers_ref):
    slots, features = answers_ref.shape
    devices = labels.shape[0]
    sender = floor_div(iota((slots, devices), 0), capacity) == iota((slots, devices), 1)
    filled = dot_t(jnp.where(sender, 1.0, 0.0).astype(BF16), lanes_of(labels, per_device, per_device))
    row = iota((slots, 1), 0)
    place = (row - floor_div(row, capacity) * capacity).astype(F32)
    reads, begin = [], jnp.zeros((slots, 1), F32)
    for block in range(per_device):
        end = begin + filled[:, block : block + 1]
        here = jnp.where((place >= begin) & (place < end), 1.0, 0.0)
        reads.append(jnp.broadcast_to(here, (slots, BLOCK)))
        begin = end

    @pl.loop(0, features // LANES, unroll=unroll)
    def _(pair):
        columns = pl.ds(pl.multiple_of(pair * LANES, LANES), LANES)
        second = pl.ds(pl.multiple_of(features + pair * LANES, LANES), LANES)
        queries = queries_ref[:, columns]
        even = even_lanes((slots, LANES), head_size)
        outputs = []
        for head in range(LANES // head_size):
            picked = jnp.where(even if head == 0 else ~even, queries, jnp.zeros_like(queries))
            scores = dot_t(picked, other[:, columns])
            chosen_scores = scores[:, :BLOCK]
            for block in range(1, per_device):
                here = scores[:, block * BLOCK : (block + 1) * BLOCK]
                chosen_scores = jnp.where(reads[block] > 0.5, here, chosen_scores)
            powers = jnp.exp(chosen_scores - jnp.max(chosen_scores, axis=-1, keepdims=True))
            sums = jnp.sum(powers, axis=-1, keepdims=True)
            spread = jnp.concatenate(
                [jnp.where(reads[block] > 0.5, powers, 0.0).astype(BF16) for block in range(per_device)], axis=1
            )
            outputs.append(dot(spread, other[:, second]) / sums)
        answers_ref[:, columns] = jnp.where(even, outputs[0], outputs[1]).astype(BF16)


def unpack_kernel(replies_ref, back_ref, out_w, update_hbm, decoded, update_ref, sent):
    features = out_w.shape[1]
    decoded[...] = dot(back_ref[...], replies_ref[...]).astype(BF16)
    copies = []
    for i in range(features // TILE):
        columns = pl.ds(i * TILE, TILE)
        update_ref[:, columns] = dot(decoded[...], out_w[:, columns]).astype(BF16)
        copies.append(pltpu.make_async_copy(update_ref.at[:, columns], update_hbm.at[:, columns], sent.at[i]))
        copies[-1].start()
    for copy in copies:
        copy.wait()


def call(kernel, operands, outs, scratch, name, flops, limit=VMEM_MIB, out_space=VMEM):
    return pl.pallas_call(
        kernel,
        out_shape=[jax.ShapeDtypeStruct(*out) if isinstance(out, tuple) else out for out in outs],
        in_specs=[pl.BlockSpec(memory_space=space) for space, _ in operands],
        out_specs=[pl.BlockSpec(memory_space=out_space) for _ in outs],
        scratch_shapes=scratch,
        name=name,
        cost_estimate=pl.CostEstimate(flops=flops, bytes_accessed=4 * MIB, transcendentals=0),
        compiler_params=pltpu.CompilerParams(vmem_limit_bytes=limit * MIB),
    )(*[pltpu.with_memory_space_constraint(value, HBM) if space is HBM else value for space, value in operands])


def held_like(*values):
    return [*[VMEM(value.shape, value.dtype) for value in values], pltpu.SemaphoreType.DMA((len(values),))]


def weights_held(count, features):
    return [VMEM((count, features, TILE), BF16), pltpu.SemaphoreType.DMA((count,))]


def on_device(
    grid_state,
    mesh_state,
    encode_block,
    neighbour_block,
    decode_block,
    encode_grid_gain,
    encode_mesh_gain,
    process_gain,
    decode_grid_gain,
    decode_mesh_gain,
    encode_query,
    encode_keyval,
    encode_out,
    process_qkv,
    process_out,
    decode_query,
    decode_keyval,
    decode_out,
):
    devices = lax.axis_size(AXES)
    me = lax.axis_index(AXES)
    grid_count, features = grid_state.shape
    mesh_rows = mesh_state.shape[0]
    per_device = mesh_rows // BLOCK
    total_blocks = per_device * devices
    capacity = max(4, 2 * grid_count // devices)
    slots = devices * capacity
    head_size = features // HEADS
    scale = head_size ** (-0.5)
    tiles = features // TILE
    me_row = me.astype(jnp.int32).reshape(1)
    encode_row, decode_row = encode_block.reshape(1, -1), decode_block.reshape(1, -1)
    encode_grid_gain, encode_mesh_gain, process_gain, decode_grid_gain, decode_mesh_gain = [
        gain.reshape(1, -1)
        for gain in (encode_grid_gain, encode_mesh_gain, process_gain, decode_grid_gain, decode_mesh_gain)
    ]

    def exchange(rows, *shape):
        return lax.all_to_all(rows.reshape(devices, *shape), AXES, split_axis=0, concat_axis=0, tiled=True)

    if by_tiles(capacity):
        payload = (capacity * features // LANES + 8, LANES)
        packed_shape = (devices, *payload)
    else:
        payload = (capacity, features + LANES)
        packed_shape = (slots, features + LANES)
    (packed,) = call(
        functools.partial(fill_kernel, devices, per_device, capacity),
        [(HBM, grid_state), (HBM, encode_row), (HBM, decode_row), (HBM, encode_grid_gain)],
        [(packed_shape, BF16)],
        [
            *held_like(grid_state, encode_row, decode_row, encode_grid_gain),
            VMEM(packed_shape, BF16),
            pltpu.SemaphoreType.DMA((features // LANES + 1,)),
        ],
        "fill",
        flops=600_000_000,
        out_space=ANY,
    )
    received = exchange(packed, *payload).reshape(packed_shape)
    query, packed_queries, back = call(
        functools.partial(query_kernel, devices, per_device, capacity, scale),
        [
            (HBM, mesh_state), (HBM, encode_mesh_gain), (HBM, encode_query),
            (HBM, grid_state), (HBM, decode_grid_gain), (HBM, decode_query), (HBM, decode_row),
        ],
        [((mesh_rows, features), BF16), ((slots, features), BF16), ((grid_count, slots), BF16)],
        [
            *held_like(mesh_state, encode_mesh_gain, grid_state, decode_grid_gain, decode_row),
            VMEM((grid_count, features), BF16),
            *weights_held(2 * tiles, features),
        ],
        "queries",
        flops=2_000_000_000,
    )
    arrived_queries = exchange(packed_queries, capacity, features).reshape(slots, features)
    mesh_mid, process_norm, labels = call(
        functools.partial(encode_kernel, per_device, capacity, head_size, ENCODE_UNROLL),
        [
            (ANY, received), (HBM, query), (HBM, mesh_state), (HBM, process_gain),
            (HBM, encode_keyval), (HBM, encode_out),
        ],
        [((mesh_rows, features), BF16), ((mesh_rows, features), BF16), ((devices, LANES), BF16)],
        [
            *held_like(received, query, mesh_state, process_gain),
            VMEM((slots, features), BF16),
            VMEM((slots, 2 * features), BF16),
            VMEM((mesh_rows, features), BF16),
            VMEM((8, slots), F32),
            *weights_held(3 * tiles, features),
        ],
        "encode",
        flops=5_000_000_000,
    )
    pairs = [(i, i ^ 1) for i in range(devices)]
    across = [(i, i + 1 if i % 2 else i - 1) for i in range(1, devices - 1)]
    first = lax.ppermute(process_norm, AXES, pairs)
    second = lax.ppermute(process_norm, AXES, across)
    (mesh_qkv,) = call(
        functools.partial(own_kernel, scale),
        [(HBM, process_norm), (HBM, process_qkv)],
        [((mesh_rows, 3 * features), BF16)],
        [
            *held_like(process_norm),
            VMEM((3 * tiles, features, TILE), BF16),
            pltpu.SemaphoreType.DMA((3 * tiles,)),
        ],
        "own",
        flops=2_000_000_000,
    )
    kv_w, out_w, decode_w, mesh_qkv, mesh_mid, arrived_queries = call(
        hold_kernel,
        [
            (HBM, process_qkv), (HBM, process_out), (HBM, decode_keyval),
            (HBM, mesh_qkv), (HBM, mesh_mid), (ANY, arrived_queries),
        ],
        [
            *[VMEM((count * tiles, features, TILE), BF16) for count in (2, 1, 2)],
            *[VMEM(rows.shape, BF16) for rows in (mesh_qkv, mesh_mid, arrived_queries)],
        ],
        [pltpu.SemaphoreType.DMA((3,)), pltpu.SemaphoreType.DMA((5 * tiles,))],
        "hold",
        flops=2_000_000_000,
        limit=36,
    )
    (answers,) = call(
        functools.partial(process_kernel, per_device, capacity, head_size, PROCESS_UNROLL, DECODE_UNROLL),
        [
            (SMEM, me_row), (SMEM, neighbour_block), (ANY, first), (ANY, process_norm), (ANY, second),
            (VMEM, mesh_qkv), (VMEM, mesh_mid), (HBM, decode_mesh_gain), (VMEM, arrived_queries), (HBM, labels),
            (VMEM, kv_w), (VMEM, out_w), (VMEM, decode_w),
        ],
        [((slots, features), BF16)],
        [
            *held_like(decode_mesh_gain, labels),
            pltpu.SemaphoreType.DMA((per_device,)),
            VMEM((mesh_rows, features), BF16),
            VMEM((mesh_rows, 2 * features), BF16),
            VMEM((mesh_rows, features), BF16),
            VMEM((mesh_rows, features), BF16),
        ],
        "process",
        flops=8_000_000_000,
        limit=36,
    )
    replies = exchange(answers, capacity, features).reshape(slots, features)
    (update,) = call(
        unpack_kernel,
        [(VMEM, replies), (VMEM, back), (VMEM, decode_out)],
        [((grid_count, features), BF16)],
        [
            VMEM((grid_count, features), BF16),
            VMEM((grid_count, features), BF16),
            pltpu.SemaphoreType.DMA((tiles,)),
        ],
        "unpack",
        flops=1_000_000_000,
        limit=24,
        out_space=ANY,
    )
    return update


def solution(mesh):
    in_specs = (P(AXES, None), P(AXES, None), P(AXES), P(AXES), P(AXES), *[P()] * 13)
    return jax.shard_map(
        on_device, mesh=mesh, in_specs=in_specs, out_specs=P(AXES, None), check_vma=False
    )
```

```python
import functools

import jax
import jax.numpy as jnp
from jax import lax
from jax.experimental import pallas as pl
from jax.experimental.pallas import tpu as pltpu
from jax.sharding import PartitionSpec as P

HEADS = 16
BLOCK = 128
TILE = 512
LANES = 128
MASKED = -1e30
VMEM_MIB = 56
PARTS = 4
ENCODE_UNROLL = 4
PROCESS_UNROLL = 8
DECODE_UNROLL = 8
ANY, HBM, VMEM, SMEM = pl.ANY, pltpu.HBM, pltpu.VMEM, pltpu.SMEM
AXES = ("gx", "gy")
F32 = jnp.float32
BF16 = jnp.bfloat16
MIB = 1024 * 1024


def iota(shape, dim):
    return lax.broadcasted_iota(jnp.int32, shape, dim)


def floor_div(values, by):
    return jnp.floor((values.astype(F32) + 0.5) * (1.0 / by)).astype(jnp.int32)


def dot(left, right):
    return jnp.dot(left, right, preferred_element_type=F32)


def dot_t(left, right):
    return lax.dot_general(left, right, (((1,), (1,)), ((), ())), preferred_element_type=F32)


def dot_tl(left, right):
    return lax.dot_general(left, right, (((0,), (0,)), ((), ())), preferred_element_type=F32)


def normed(values, gain):
    wide = values.astype(F32)
    return wide * lax.rsqrt(jnp.mean(wide * wide, axis=-1, keepdims=True) + 1e-06) * gain


def block_hits(blocks, total_blocks):
    hits = iota((total_blocks, blocks.shape[1]), 0) == blocks
    return jnp.where(hits, 1.0, 0.0).astype(F32)


def block_counts(hits):
    counts = jnp.sum(hits, axis=1, keepdims=True)
    return jnp.broadcast_to(counts, (hits.shape[0], LANES)).astype(BF16)


def slots_of(hits, per_device, capacity):
    total_blocks, points = hits.shape
    earlier = jnp.where(iota((points, points), 0) < iota((points, points), 1), 1.0, 0.0)
    before = dot(hits.astype(BF16), earlier.astype(BF16))
    row, column = iota((total_blocks, total_blocks), 0), iota((total_blocks, total_blocks), 1)
    mates = (floor_div(row, per_device) == floor_div(column, per_device)) & (column < row)
    offset = dot(jnp.where(mates, 1.0, 0.0).astype(BF16), block_counts(hits))[:, :1]
    owner = floor_div(iota((total_blocks, 1), 0), per_device)
    base = owner.astype(F32) * capacity + offset
    return jnp.sum(hits * (base + before), axis=0, keepdims=True).astype(jnp.int32)


def placement(slot, slots):
    return jnp.where(iota((slots, slot.shape[1]), 0) == slot, 1.0, 0.0).astype(BF16)


class Fetch:
    def __init__(self, source, held, ready):
        self.copy = pltpu.make_async_copy(source, held, ready)
        self.held = held
        self.waiting = True
        self.copy.start()

    def __call__(self):
        if self.waiting:
            self.copy.wait()
            self.waiting = False
        return self.held


class Weight:
    def __init__(self, source, held, ready, base, count, first=0, semaphore=None):
        semaphore = base if semaphore is None else semaphore
        self.source, self.held, self.ready, self.base, self.count = source, held, ready, base, count
        self.semaphore = semaphore

        @pl.loop(0, count)
        def _(i):
            columns = pl.ds(pl.multiple_of((first + i) * TILE, TILE), TILE)
            pltpu.make_async_copy(source.at[:, columns], held.at[base + i], ready.at[semaphore + i]).start()

    def arrive(self, i):
        held = self.held.at[self.base + i]
        pltpu.make_async_copy(self.source.at[:, pl.ds(0, TILE)], held, self.ready.at[self.semaphore + i]).wait()
        return held

    def wait(self):
        @pl.loop(0, self.count)
        def _(i):
            self.arrive(i)

    def product(self, rows, put):
        for i in range(self.count):
            put(pl.ds(i * TILE, TILE), dot(rows[...], self.arrive(i)[...]))


def product(rows, held, put):
    for i in range(held.shape[0]):
        put(pl.ds(i * TILE, TILE), dot(rows[...], held[i]))


def store_in(ref):
    def put(columns, values):
        ref[:, columns] = values.astype(ref.dtype)

    return put


def count_lanes(encode_counts, decode_counts, devices, per_device):
    total_blocks = encode_counts.shape[0]
    lane = iota((devices, LANES), 1)
    labels = jnp.zeros((devices, LANES), F32)
    for kind, counts in enumerate((encode_counts, decode_counts)):
        for block in range(per_device):
            wanted = iota((devices, total_blocks), 0) * per_device + block
            wanted = jnp.where(iota((devices, total_blocks), 1) == wanted, 1.0, 0.0).astype(BF16)
            labels = labels + jnp.where(lane == kind * per_device + block, dot(wanted, counts), 0.0)
    return labels.astype(BF16)


def by_tiles(capacity):
    return capacity % 16 == 0


def fill_kernel(
    devices, per_device, capacity,
    state_hbm, encode_hbm, decode_hbm, gain_hbm, packed_hbm,
    state_held, encode_held, decode_held, gain_held, ready, packed_ref, sent,
):
    encode = Fetch(encode_hbm, encode_held, ready.at[0])
    decode = Fetch(decode_hbm, decode_held, ready.at[1])
    state = Fetch(state_hbm, state_held, ready.at[2])
    gain = Fetch(gain_hbm, gain_held, ready.at[3])
    total_blocks, slots = devices * per_device, devices * capacity
    encode_hits = block_hits(encode()[...], total_blocks)
    place = placement(slots_of(encode_hits, per_device, capacity), slots)
    decode_hits = block_hits(decode()[...], total_blocks)
    labels = count_lanes(block_counts(encode_hits), block_counts(decode_hits), devices, per_device)
    norm = normed(state()[...], gain()[...]).astype(BF16)
    features = norm.shape[1]
    copies = []

    def send(place):
        copies.append(pltpu.make_async_copy(packed_ref.at[place], packed_hbm.at[place], sent.at[len(copies)]))
        copies[-1].start()

    if by_tiles(capacity):
        last = pl.ds(features // LANES * capacity, 8)
        packed_ref[:, last] = jnp.broadcast_to(labels[:, None, :], (devices, 8, LANES))
        part = devices // PARTS
        for i in range(PARTS):
            owners = pl.ds(i * part, part)
            rows = dot(place[i * part * capacity : (i + 1) * part * capacity], norm).astype(BF16)
            for tile in range(features // LANES):
                columns = rows[:, tile * LANES : (tile + 1) * LANES].reshape(part, capacity, LANES)
                packed_ref[owners, pl.ds(tile * capacity, capacity)] = columns
            send(owners)
    else:
        packed_ref[:, pl.ds(0, features)] = dot(place, norm).astype(BF16)
        owner = floor_div(iota((slots, devices), 0), capacity) == iota((slots, devices), 1)
        packed_ref[:, pl.ds(features, LANES)] = dot(jnp.where(owner, 1.0, 0.0).astype(BF16), labels).astype(BF16)
        send(slice(None))
    for copy in copies:
        copy.wait()


def query_kernel(
    devices, per_device, capacity, scale,
    mesh_hbm, mesh_gain_hbm, encode_w, grid_hbm, grid_gain_hbm, decode_w, decode_hbm,
    query_ref, packed_ref, back_ref,
    mesh_held, mesh_gain_held, grid_held, grid_gain_held, decode_held, ready,
    norm_ref, weights, arrived,
):
    decode = Fetch(decode_hbm, decode_held, ready.at[0])
    grid = Fetch(grid_hbm, grid_held, ready.at[1])
    grid_gain = Fetch(grid_gain_hbm, grid_gain_held, ready.at[2])
    mesh = Fetch(mesh_hbm, mesh_held, ready.at[3])
    mesh_gain = Fetch(mesh_gain_hbm, mesh_gain_held, ready.at[4])
    count = encode_w.shape[1] // TILE
    decode_weight = Weight(decode_w, weights, arrived, 0, count)
    encode_weight = Weight(encode_w, weights, arrived, count, count)
    slots = packed_ref.shape[0]
    hits = block_hits(decode()[...], devices * per_device)
    place = placement(slots_of(hits, per_device, capacity), slots)
    back_ref[...] = place.T
    norm_ref[...] = normed(grid()[...], grid_gain()[...]).astype(BF16)

    def put_packed(columns, values):
        rounded = (values.astype(BF16).astype(F32) * scale).astype(BF16)
        packed_ref[:, columns] = dot(place, rounded).astype(BF16)

    decode_weight.product(norm_ref, put_packed)
    norm_ref[...] = normed(mesh()[...], mesh_gain()[...]).astype(BF16)

    def put_query(columns, values):
        query_ref[:, columns] = (values.astype(BF16).astype(F32) * scale).astype(BF16)

    encode_weight.product(norm_ref, put_query)


def lanes_of(labels, first, count):
    row, lane = iota((8, LANES), 0), iota((8, LANES), 1)
    wanted = (lane == row + first) & (row < count)
    return dot_t(jnp.where(wanted, 1.0, 0.0).astype(BF16), labels).astype(BF16)


def even_lanes(shape, head_size):
    return iota(shape, len(shape) - 1) < head_size


def split_heads(values, head_size):
    even = even_lanes(values.shape, head_size)
    zero = jnp.zeros_like(values)
    return jnp.concatenate([jnp.where(even, values, zero), jnp.where(even, zero, values)], axis=0)


def join_heads(values, head_size):
    rows = values.shape[0] // 2
    even = even_lanes((rows, values.shape[1]), head_size)
    return jnp.where(even, values[:rows], values[rows:])


def share_out(powers, values):
    output = dot(powers.astype(BF16), jnp.concatenate([values, jnp.ones_like(values)], axis=1))
    return output[:, :LANES] / output[:, LANES:]


def keys_first(scores):
    powers = jnp.exp(scores - jnp.max(scores, axis=0, keepdims=True))
    return powers.astype(BF16), 1.0 / jnp.sum(powers, axis=0, keepdims=True)


def encode_kernel(
    per_device, capacity, head_size, unroll,
    received_hbm, query_hbm, mesh_hbm, gain_hbm, keyval_w, out_w,
    mid_ref, norm_ref, labels_ref,
    received_held, query_held, mesh_held, gain_held, ready,
    rows_ref, keyval, attended, bias, weights, arrived,
):
    features = mid_ref.shape[1]
    devices = labels_ref.shape[0]
    slots = devices * capacity
    kv_count, out_count = keyval_w.shape[1] // TILE, features // TILE
    received = Fetch(received_hbm, received_held, ready.at[0])
    keyval_weight = Weight(keyval_w, weights, arrived, 0, kv_count)
    query_rows = Fetch(query_hbm, query_held, ready.at[1])
    out_weight = Weight(out_w, weights, arrived, kv_count, out_count)
    mesh = Fetch(mesh_hbm, mesh_held, ready.at[2])
    gain = Fetch(gain_hbm, gain_held, ready.at[3])
    received_ref = received()
    if by_tiles(capacity):
        for tile in range(features // LANES):
            part = received_ref[:, pl.ds(tile * capacity, capacity), :]
            rows_ref[:, pl.ds(tile * LANES, LANES)] = part.reshape(slots, LANES)
        last = received_ref[:, pl.ds(features // LANES * capacity, 8), :]
        labels = jnp.max(last.astype(F32), axis=1).astype(BF16)
        rows = rows_ref
    else:
        rows = received_ref.at[:, pl.ds(0, features)]
        first = iota((devices, slots), 1) == iota((devices, slots), 0) * capacity
        labels = dot(jnp.where(first, 1.0, 0.0).astype(BF16), received_ref[:, pl.ds(features, LANES)]).astype(BF16)
    labels_ref[...] = labels
    keyval_weight.product(rows, store_in(keyval))

    sender = floor_div(iota((devices, slots), 1), capacity) == iota((devices, slots), 0)
    filled = dot(lanes_of(labels, 0, per_device), jnp.where(sender, 1.0, 0.0).astype(BF16))
    lane = iota((1, slots), 1)
    place = (lane - floor_div(lane, capacity) * capacity).astype(F32)
    begin = jnp.zeros((1, slots), F32)
    for block in range(per_device):
        end = begin + filled[block : block + 1]
        bias[block : block + 1] = jnp.where((place >= begin) & (place < end), 0.0, MASKED)
        begin = end
    query_ref = query_rows()

    @pl.loop(0, features // LANES, unroll=unroll)
    def _(pair):
        columns = pl.ds(pl.multiple_of(pair * LANES, LANES), LANES)
        value_columns = pl.ds(pl.multiple_of(features + pair * LANES, LANES), LANES)
        keys, values = keyval[:, columns], keyval[:, value_columns]
        for block in range(per_device):
            block_rows = pl.ds(block * BLOCK, BLOCK)
            queries = split_heads(query_ref[block_rows, columns], head_size)
            scores = dot_t(queries, keys) + bias[block : block + 1]
            powers = jnp.exp(scores - jnp.max(scores, axis=-1, keepdims=True))
            output = share_out(powers, values)
            attended[block_rows, columns] = join_heads(output, head_size).astype(BF16)

    mesh_ref = mesh()

    def put_mid(columns, values):
        mid_ref[:, columns] = (mesh_ref[:, columns].astype(F32) + values).astype(BF16)

    out_weight.product(attended, put_mid)
    norm_ref[...] = normed(mid_ref[...], gain()[...]).astype(BF16)


def own_kernel(scale, norm_hbm, qkv_w, qkv_ref, norm_held, ready, qkv_held, arrived):
    features = norm_hbm.shape[1]
    norm = Fetch(norm_hbm, norm_held, ready.at[0])
    weight = Weight(qkv_w, qkv_held, arrived, 0, qkv_held.shape[0])
    weight.product(norm(), store_in(qkv_ref))
    queries = pl.ds(0, features)
    qkv_ref[:, queries] = (qkv_ref[:, queries].astype(F32) * scale).astype(BF16)


def hold_kernel(
    qkv_w, out_w, decode_w, qkv_hbm, after_hbm, kv_kept, out_kept, decode_kept, qkv_kept, ready, arrived
):
    tiles = out_kept.shape[0]
    weights = [
        Weight(qkv_w, kv_kept, arrived, 0, 2 * tiles, tiles),
        Weight(out_w, out_kept, arrived, 0, tiles, 0, 2 * tiles),
        Weight(decode_w, decode_kept, arrived, 0, 2 * tiles, 0, 3 * tiles),
    ]
    qkv = Fetch(qkv_hbm, qkv_kept, ready.at[0])
    for weight in weights:
        weight.wait()
    qkv()


def process_kernel(
    per_device, capacity, head_size, unroll, decode_unroll,
    me_ref, neighbour_ref, first_hbm, norm_hbm, second_hbm, qkv_ref, mid_hbm, gain_hbm, queries_ref, labels_hbm,
    kv_w, out_w, decode_w,
    answers_ref,
    mid_held, gain_held, labels_held, ready, picked,
    chosen, other, attended, mesh_out,
):
    features = mid_hbm.shape[1]
    odd = me_ref[0] % 2
    for block in range(per_device):
        rows = pl.ds(block * BLOCK, BLOCK)
        position = neighbour_ref[block] - me_ref[0] * per_device + per_device
        sides = ((first_hbm, 2 * (1 - odd)), (norm_hbm, 1), (second_hbm, 2 * odd))
        for source, side in sides:
            for place in range(per_device):
                @pl.when(position == side * per_device + place)
                def _():
                    block_rows = source.at[pl.ds(place * BLOCK, BLOCK)]
                    pltpu.make_async_copy(block_rows, chosen.at[rows], picked.at[block]).start()

    mid = Fetch(mid_hbm, mid_held, ready.at[0])
    gain = Fetch(gain_hbm, gain_held, ready.at[1])
    labels = Fetch(labels_hbm, labels_held, ready.at[2])
    for block in range(per_device):
        rows = pl.ds(block * BLOCK, BLOCK)
        pltpu.make_async_copy(norm_hbm.at[rows], chosen.at[rows], picked.at[block]).wait()
    product(chosen, kv_w, store_in(other))

    @pl.loop(0, features // LANES, unroll=unroll)
    def _(pair):
        columns = pl.ds(pl.multiple_of(pair * LANES, LANES), LANES)
        second = pl.ds(pl.multiple_of(features + pair * LANES, LANES), LANES)
        third = pl.ds(pl.multiple_of(2 * features + pair * LANES, LANES), LANES)
        for block in range(per_device):
            rows = pl.ds(block * BLOCK, BLOCK)
            queries = split_heads(qkv_ref[rows, columns], head_size)
            keys = jnp.concatenate([qkv_ref[rows, second], other[rows, columns]], axis=0)
            values = jnp.concatenate([qkv_ref[rows, third], other[rows, second]], axis=0)
            scores = dot_t(queries, keys)
            powers = jnp.exp(scores - jnp.max(scores, axis=-1, keepdims=True))
            sums = jnp.sum(powers, axis=-1, keepdims=True)
            output = dot(powers.astype(BF16), values) / sums
            attended[rows, columns] = join_heads(output, head_size).astype(BF16)

    mid_ref = mid()

    def put_out(columns, values):
        mesh_out[:, columns] = (mid_ref[:, columns].astype(F32) + values).astype(BF16)

    product(attended, out_w, put_out)
    chosen[...] = normed(mesh_out[...], gain()[...]).astype(BF16)
    product(chosen, decode_w, store_in(other))
    decode_points(
        per_device, capacity, head_size, decode_unroll, other, queries_ref, labels()[...], answers_ref
    )


def decode_points(per_device, capacity, head_size, unroll, other, queries_ref, labels, answers_ref):
    slots, features = answers_ref.shape
    devices = labels.shape[0]
    sender = floor_div(iota((slots, devices), 0), capacity) == iota((slots, devices), 1)
    filled = dot_t(jnp.where(sender, 1.0, 0.0).astype(BF16), lanes_of(labels, per_device, per_device))
    row = iota((slots, 1), 0)
    place = (row - floor_div(row, capacity) * capacity).astype(F32)
    reads, begin = [], jnp.zeros((slots, 1), F32)
    for block in range(per_device):
        end = begin + filled[:, block : block + 1]
        here = jnp.where((place >= begin) & (place < end), 1.0, 0.0)
        reads.append(jnp.broadcast_to(here, (slots, LANES)) > 0.5)
        begin = end

    @pl.loop(0, features // LANES, unroll=unroll)
    def _(pair):
        columns = pl.ds(pl.multiple_of(pair * LANES, LANES), LANES)
        second = pl.ds(pl.multiple_of(features + pair * LANES, LANES), LANES)
        queries = queries_ref[:, columns]
        even = even_lanes((slots, LANES), head_size)
        zero = jnp.zeros_like(queries)
        spread = jnp.concatenate([jnp.where(here, queries, zero) for here in reads], axis=1)
        keys, values = [
            jnp.concatenate(
                [split_heads(other[pl.ds(block * BLOCK, BLOCK), side], head_size) for block in range(per_device)], axis=1
            )
            for side in (columns, second)
        ]
        scores = dot_t(spread, keys)
        powers, sums = [], []
        for head in range(2):
            here = scores[:, head * BLOCK : (head + 1) * BLOCK]
            powers.append(jnp.exp(here - jnp.max(here, axis=-1, keepdims=True)))
            sums.append(jnp.sum(powers[head], axis=-1, keepdims=True))
        output = dot(jnp.concatenate(powers, axis=1).astype(BF16), values)
        answer = output[:, :LANES]
        for block in range(1, per_device):
            answer = jnp.where(reads[block], output[:, block * LANES : (block + 1) * LANES], answer)
        answers_ref[:, columns] = (answer / jnp.where(even, sums[0], sums[1])).astype(BF16)


def unpack_kernel(replies_ref, back_ref, out_w, update_hbm, decoded, update_ref, sent):
    features = out_w.shape[1]
    decoded[...] = dot(back_ref[...], replies_ref[...]).astype(BF16)
    copies = []
    for i in range(features // TILE):
        columns = pl.ds(i * TILE, TILE)
        update_ref[:, columns] = dot(decoded[...], out_w[:, columns]).astype(BF16)
        copies.append(pltpu.make_async_copy(update_ref.at[:, columns], update_hbm.at[:, columns], sent.at[i]))
        copies[-1].start()
    for copy in copies:
        copy.wait()


def call(kernel, operands, outs, scratch, name, flops, limit=VMEM_MIB, out_space=VMEM):
    return pl.pallas_call(
        kernel,
        out_shape=[jax.ShapeDtypeStruct(*out) if isinstance(out, tuple) else out for out in outs],
        in_specs=[pl.BlockSpec(memory_space=space) for space, _ in operands],
        out_specs=[pl.BlockSpec(memory_space=out_space) for _ in outs],
        scratch_shapes=scratch,
        name=name,
        cost_estimate=pl.CostEstimate(flops=flops, bytes_accessed=4 * MIB, transcendentals=0),
        compiler_params=pltpu.CompilerParams(vmem_limit_bytes=limit * MIB),
    )(*[pltpu.with_memory_space_constraint(value, HBM) if space is HBM else value for space, value in operands])


def held_like(*values):
    return [*[VMEM(value.shape, value.dtype) for value in values], pltpu.SemaphoreType.DMA((len(values),))]


def weights_held(count, features):
    return [VMEM((count, features, TILE), BF16), pltpu.SemaphoreType.DMA((count,))]


def on_device(
    grid_state,
    mesh_state,
    encode_block,
    neighbour_block,
    decode_block,
    encode_grid_gain,
    encode_mesh_gain,
    process_gain,
    decode_grid_gain,
    decode_mesh_gain,
    encode_query,
    encode_keyval,
    encode_out,
    process_qkv,
    process_out,
    decode_query,
    decode_keyval,
    decode_out,
):
    devices = lax.axis_size(AXES)
    me = lax.axis_index(AXES)
    grid_count, features = grid_state.shape
    mesh_rows = mesh_state.shape[0]
    per_device = mesh_rows // BLOCK
    total_blocks = per_device * devices
    capacity = max(4, 2 * grid_count // devices)
    slots = devices * capacity
    head_size = features // HEADS
    scale = head_size ** (-0.5)
    tiles = features // TILE
    me_row = me.astype(jnp.int32).reshape(1)
    encode_row, decode_row = encode_block.reshape(1, -1), decode_block.reshape(1, -1)
    encode_grid_gain, encode_mesh_gain, process_gain, decode_grid_gain, decode_mesh_gain = [
        gain.reshape(1, -1)
        for gain in (encode_grid_gain, encode_mesh_gain, process_gain, decode_grid_gain, decode_mesh_gain)
    ]

    def exchange(rows, *shape):
        return lax.all_to_all(rows.reshape(devices, *shape), AXES, split_axis=0, concat_axis=0, tiled=True)

    if by_tiles(capacity):
        payload = (capacity * features // LANES + 8, LANES)
        packed_shape = (devices, *payload)
    else:
        payload = (capacity, features + LANES)
        packed_shape = (slots, features + LANES)
    (packed,) = call(
        functools.partial(fill_kernel, devices, per_device, capacity),
        [(HBM, grid_state), (HBM, encode_row), (HBM, decode_row), (HBM, encode_grid_gain)],
        [(packed_shape, BF16)],
        [
            *held_like(grid_state, encode_row, decode_row, encode_grid_gain),
            VMEM(packed_shape, BF16),
            pltpu.SemaphoreType.DMA((PARTS,)),
        ],
        "fill",
        flops=600_000_000,
        out_space=ANY,
    )
    received = exchange(packed, *payload).reshape(packed_shape)
    query, packed_queries, back = call(
        functools.partial(query_kernel, devices, per_device, capacity, scale),
        [
            (HBM, mesh_state), (HBM, encode_mesh_gain), (HBM, encode_query),
            (HBM, grid_state), (HBM, decode_grid_gain), (HBM, decode_query), (HBM, decode_row),
        ],
        [((mesh_rows, features), BF16), ((slots, features), BF16), ((grid_count, slots), BF16)],
        [
            *held_like(mesh_state, encode_mesh_gain, grid_state, decode_grid_gain, decode_row),
            VMEM((grid_count, features), BF16),
            *weights_held(2 * tiles, features),
        ],
        "queries",
        flops=2_000_000_000,
    )
    arrived_queries = exchange(packed_queries, capacity, features).reshape(slots, features)
    mesh_mid, process_norm, labels = call(
        functools.partial(encode_kernel, per_device, capacity, head_size, ENCODE_UNROLL),
        [
            (ANY, received), (HBM, query), (HBM, mesh_state), (HBM, process_gain),
            (HBM, encode_keyval), (HBM, encode_out),
        ],
        [((mesh_rows, features), BF16), ((mesh_rows, features), BF16), ((devices, LANES), BF16)],
        [
            *held_like(received, query, mesh_state, process_gain),
            VMEM((slots, features), BF16),
            VMEM((slots, 2 * features), BF16),
            VMEM((mesh_rows, features), BF16),
            VMEM((8, slots), F32),
            *weights_held(3 * tiles, features),
        ],
        "encode",
        flops=5_000_000_000,
    )
    pairs = [(i, i ^ 1) for i in range(devices)]
    across = [(i, i + 1 if i % 2 else i - 1) for i in range(1, devices - 1)]
    first = lax.ppermute(process_norm, AXES, pairs)
    second = lax.ppermute(process_norm, AXES, across)
    (mesh_qkv,) = call(
        functools.partial(own_kernel, scale),
        [(HBM, process_norm), (HBM, process_qkv)],
        [((mesh_rows, 3 * features), BF16)],
        [
            *held_like(process_norm),
            VMEM((3 * tiles, features, TILE), BF16),
            pltpu.SemaphoreType.DMA((3 * tiles,)),
        ],
        "own",
        flops=2_000_000_000,
    )
    kv_w, out_w, decode_w, mesh_qkv = call(
        hold_kernel,
        [(HBM, process_qkv), (HBM, process_out), (HBM, decode_keyval), (HBM, mesh_qkv), (ANY, arrived_queries)],
        [
            *[VMEM((count * tiles, features, TILE), BF16) for count in (2, 1, 2)],
            VMEM(mesh_qkv.shape, BF16),
        ],
        [pltpu.SemaphoreType.DMA((1,)), pltpu.SemaphoreType.DMA((5 * tiles,))],
        "hold",
        flops=2_000_000_000,
        limit=36,
    )
    (answers,) = call(
        functools.partial(process_kernel, per_device, capacity, head_size, PROCESS_UNROLL, DECODE_UNROLL),
        [
            (SMEM, me_row), (SMEM, neighbour_block), (ANY, first), (ANY, process_norm), (ANY, second),
            (VMEM, mesh_qkv), (HBM, mesh_mid), (HBM, decode_mesh_gain), (VMEM, arrived_queries), (HBM, labels),
            (VMEM, kv_w), (VMEM, out_w), (VMEM, decode_w),
        ],
        [((slots, features), BF16)],
        [
            *held_like(mesh_mid, decode_mesh_gain, labels),
            pltpu.SemaphoreType.DMA((per_device,)),
            VMEM((mesh_rows, features), BF16),
            VMEM((mesh_rows, 2 * features), BF16),
            VMEM((mesh_rows, features), BF16),
            VMEM((mesh_rows, features), BF16),
        ],
        "process",
        flops=8_000_000_000,
        limit=36,
    )
    replies = exchange(answers, capacity, features).reshape(slots, features)
    (update,) = call(
        unpack_kernel,
        [(VMEM, replies), (VMEM, back), (VMEM, decode_out)],
        [((grid_count, features), BF16)],
        [
            VMEM((grid_count, features), BF16),
            VMEM((grid_count, features), BF16),
            pltpu.SemaphoreType.DMA((tiles,)),
        ],
        "unpack",
        flops=1_000_000_000,
        limit=24,
        out_space=ANY,
    )
    return update


def solution(mesh):
    in_specs = (P(AXES, None), P(AXES, None), P(AXES), P(AXES), P(AXES), *[P()] * 13)
    return jax.shard_map(
        on_device, mesh=mesh, in_specs=in_specs, out_specs=P(AXES, None), check_vma=False
    )
```

```python
import functools

import jax
import jax.numpy as jnp
from jax import lax
from jax.experimental import pallas as pl
from jax.experimental.pallas import tpu as pltpu
from jax.sharding import PartitionSpec as P

HEADS = 16
BLOCK = 128
TILE = 512
LANES = 128
MASKED = -1e30
VMEM_MIB = 56
PARTS = 4
ENCODE_UNROLL = 8
PROCESS_UNROLL = 8
DECODE_UNROLL = 8
ANY, HBM, VMEM, SMEM = pl.ANY, pltpu.HBM, pltpu.VMEM, pltpu.SMEM
AXES = ("gx", "gy")
F32 = jnp.float32
BF16 = jnp.bfloat16
MIB = 1024 * 1024


def iota(shape, dim):
    return lax.broadcasted_iota(jnp.int32, shape, dim)


def floor_div(values, by):
    return jnp.floor((values.astype(F32) + 0.5) * (1.0 / by)).astype(jnp.int32)


def dot(left, right):
    return jnp.dot(left, right, preferred_element_type=F32)


def dot_t(left, right):
    return lax.dot_general(left, right, (((1,), (1,)), ((), ())), preferred_element_type=F32)


def dot_tl(left, right):
    return lax.dot_general(left, right, (((0,), (0,)), ((), ())), preferred_element_type=F32)


def normed(values, gain):
    wide = values.astype(F32)
    return wide * lax.rsqrt(jnp.mean(wide * wide, axis=-1, keepdims=True) + 1e-06) * gain


def block_hits(blocks, total_blocks):
    hits = iota((total_blocks, blocks.shape[1]), 0) == blocks
    return jnp.where(hits, 1.0, 0.0).astype(F32)


def block_counts(hits):
    counts = jnp.sum(hits, axis=1, keepdims=True)
    return jnp.broadcast_to(counts, (hits.shape[0], LANES)).astype(BF16)


def slots_of(hits, per_device, capacity):
    total_blocks, points = hits.shape
    earlier = jnp.where(iota((points, points), 0) < iota((points, points), 1), 1.0, 0.0)
    before = dot(hits.astype(BF16), earlier.astype(BF16))
    row, column = iota((total_blocks, total_blocks), 0), iota((total_blocks, total_blocks), 1)
    mates = (floor_div(row, per_device) == floor_div(column, per_device)) & (column < row)
    offset = dot(jnp.where(mates, 1.0, 0.0).astype(BF16), block_counts(hits))[:, :1]
    owner = floor_div(iota((total_blocks, 1), 0), per_device)
    base = owner.astype(F32) * capacity + offset
    return jnp.sum(hits * (base + before), axis=0, keepdims=True).astype(jnp.int32)


def placement(slot, slots):
    return jnp.where(iota((slots, slot.shape[1]), 0) == slot, 1.0, 0.0).astype(BF16)


class Fetch:
    def __init__(self, source, held, ready):
        self.copy = pltpu.make_async_copy(source, held, ready)
        self.held = held
        self.waiting = True
        self.copy.start()

    def __call__(self):
        if self.waiting:
            self.copy.wait()
            self.waiting = False
        return self.held


class Weight:
    def __init__(self, source, held, ready, base, count, first=0, semaphore=None):
        semaphore = base if semaphore is None else semaphore
        self.source, self.held, self.ready, self.base, self.count = source, held, ready, base, count
        self.semaphore = semaphore

        @pl.loop(0, count)
        def _(i):
            columns = pl.ds(pl.multiple_of((first + i) * TILE, TILE), TILE)
            pltpu.make_async_copy(source.at[:, columns], held.at[base + i], ready.at[semaphore + i]).start()

    def arrive(self, i):
        held = self.held.at[self.base + i]
        pltpu.make_async_copy(self.source.at[:, pl.ds(0, TILE)], held, self.ready.at[self.semaphore + i]).wait()
        return held

    def wait(self):
        @pl.loop(0, self.count)
        def _(i):
            self.arrive(i)

    def product(self, rows, put):
        for i in range(self.count):
            put(pl.ds(i * TILE, TILE), dot(rows[...], self.arrive(i)[...]))


def product(rows, held, put):
    for i in range(held.shape[0]):
        put(pl.ds(i * TILE, TILE), dot(rows[...], held[i]))


def store_in(ref):
    def put(columns, values):
        ref[:, columns] = values.astype(ref.dtype)

    return put


def count_lanes(encode_counts, decode_counts, devices, per_device):
    total_blocks = encode_counts.shape[0]
    lane = iota((devices, LANES), 1)
    labels = jnp.zeros((devices, LANES), F32)
    for kind, counts in enumerate((encode_counts, decode_counts)):
        for block in range(per_device):
            wanted = iota((devices, total_blocks), 0) * per_device + block
            wanted = jnp.where(iota((devices, total_blocks), 1) == wanted, 1.0, 0.0).astype(BF16)
            labels = labels + jnp.where(lane == kind * per_device + block, dot(wanted, counts), 0.0)
    return labels.astype(BF16)


def by_tiles(capacity):
    return capacity % 16 == 0


def fill_kernel(
    devices, per_device, capacity,
    state_hbm, encode_hbm, decode_hbm, gain_hbm, packed_hbm,
    state_held, encode_held, decode_held, gain_held, ready, packed_ref, sent,
):
    encode = Fetch(encode_hbm, encode_held, ready.at[0])
    decode = Fetch(decode_hbm, decode_held, ready.at[1])
    state = Fetch(state_hbm, state_held, ready.at[2])
    gain = Fetch(gain_hbm, gain_held, ready.at[3])
    total_blocks, slots = devices * per_device, devices * capacity
    encode_hits = block_hits(encode()[...], total_blocks)
    place = placement(slots_of(encode_hits, per_device, capacity), slots)
    decode_hits = block_hits(decode()[...], total_blocks)
    labels = count_lanes(block_counts(encode_hits), block_counts(decode_hits), devices, per_device)
    norm = normed(state()[...], gain()[...]).astype(BF16)
    features = norm.shape[1]
    copies = []

    def send(place):
        copies.append(pltpu.make_async_copy(packed_ref.at[place], packed_hbm.at[place], sent.at[len(copies)]))
        copies[-1].start()

    if by_tiles(capacity):
        last = pl.ds(features // LANES * capacity, 8)
        packed_ref[:, last] = jnp.broadcast_to(labels[:, None, :], (devices, 8, LANES))
        part = devices // PARTS
        for i in range(PARTS):
            owners = pl.ds(i * part, part)
            rows = dot(place[i * part * capacity : (i + 1) * part * capacity], norm).astype(BF16)
            for tile in range(features // LANES):
                columns = rows[:, tile * LANES : (tile + 1) * LANES].reshape(part, capacity, LANES)
                packed_ref[owners, pl.ds(tile * capacity, capacity)] = columns
            send(owners)
    else:
        packed_ref[:, pl.ds(0, features)] = dot(place, norm).astype(BF16)
        owner = floor_div(iota((slots, devices), 0), capacity) == iota((slots, devices), 1)
        packed_ref[:, pl.ds(features, LANES)] = dot(jnp.where(owner, 1.0, 0.0).astype(BF16), labels).astype(BF16)
        send(slice(None))
    for copy in copies:
        copy.wait()


def query_kernel(
    devices, per_device, capacity, scale,
    mesh_hbm, mesh_gain_hbm, encode_w, grid_hbm, grid_gain_hbm, decode_w, decode_hbm,
    query_ref, packed_ref, back_ref,
    mesh_held, mesh_gain_held, grid_held, grid_gain_held, decode_held, ready,
    norm_ref, weights, arrived,
):
    decode = Fetch(decode_hbm, decode_held, ready.at[0])
    grid = Fetch(grid_hbm, grid_held, ready.at[1])
    grid_gain = Fetch(grid_gain_hbm, grid_gain_held, ready.at[2])
    mesh = Fetch(mesh_hbm, mesh_held, ready.at[3])
    mesh_gain = Fetch(mesh_gain_hbm, mesh_gain_held, ready.at[4])
    count = encode_w.shape[1] // TILE
    decode_weight = Weight(decode_w, weights, arrived, 0, count)
    encode_weight = Weight(encode_w, weights, arrived, count, count)
    slots = packed_ref.shape[0]
    hits = block_hits(decode()[...], devices * per_device)
    place = placement(slots_of(hits, per_device, capacity), slots)
    back_ref[...] = place.T
    norm_ref[...] = normed(grid()[...], grid_gain()[...]).astype(BF16)

    def put_packed(columns, values):
        rounded = (values.astype(BF16).astype(F32) * scale).astype(BF16)
        packed_ref[:, columns] = dot(place, rounded).astype(BF16)

    decode_weight.product(norm_ref, put_packed)
    norm_ref[...] = normed(mesh()[...], mesh_gain()[...]).astype(BF16)

    def put_query(columns, values):
        query_ref[:, columns] = (values.astype(BF16).astype(F32) * scale).astype(BF16)

    encode_weight.product(norm_ref, put_query)


def lanes_of(labels, first, count):
    row, lane = iota((8, LANES), 0), iota((8, LANES), 1)
    wanted = (lane == row + first) & (row < count)
    return dot_t(jnp.where(wanted, 1.0, 0.0).astype(BF16), labels).astype(BF16)


def even_lanes(shape, head_size):
    return iota(shape, len(shape) - 1) < head_size


def split_heads(values, head_size):
    even = even_lanes(values.shape, head_size)
    zero = jnp.zeros_like(values)
    return jnp.concatenate([jnp.where(even, values, zero), jnp.where(even, zero, values)], axis=0)


def join_heads(values, head_size):
    rows = values.shape[0] // 2
    even = even_lanes((rows, values.shape[1]), head_size)
    return jnp.where(even, values[:rows], values[rows:])


def share_out(powers, values):
    output = dot(powers.astype(BF16), jnp.concatenate([values, jnp.ones_like(values)], axis=1))
    return output[:, :LANES] / output[:, LANES:]


def keys_first(scores):
    powers = jnp.exp(scores - jnp.max(scores, axis=0, keepdims=True))
    return powers.astype(BF16), 1.0 / jnp.sum(powers, axis=0, keepdims=True)


def encode_kernel(
    per_device, capacity, head_size, unroll,
    received_hbm, query_hbm, mesh_hbm, gain_hbm, keyval_w, out_w,
    mid_ref, norm_ref, labels_ref,
    received_held, query_held, mesh_held, gain_held, ready,
    rows_ref, keyval, attended, bias, weights, arrived,
):
    features = mid_ref.shape[1]
    devices = labels_ref.shape[0]
    slots = devices * capacity
    kv_count, out_count = keyval_w.shape[1] // TILE, features // TILE
    received = Fetch(received_hbm, received_held, ready.at[0])
    keyval_weight = Weight(keyval_w, weights, arrived, 0, kv_count)
    query_rows = Fetch(query_hbm, query_held, ready.at[1])
    out_weight = Weight(out_w, weights, arrived, kv_count, out_count)
    mesh = Fetch(mesh_hbm, mesh_held, ready.at[2])
    gain = Fetch(gain_hbm, gain_held, ready.at[3])
    received_ref = received()
    if by_tiles(capacity):
        for tile in range(features // LANES):
            part = received_ref[:, pl.ds(tile * capacity, capacity), :]
            rows_ref[:, pl.ds(tile * LANES, LANES)] = part.reshape(slots, LANES)
        last = received_ref[:, pl.ds(features // LANES * capacity, 8), :]
        labels = jnp.max(last.astype(F32), axis=1).astype(BF16)
        rows = rows_ref
    else:
        rows = received_ref.at[:, pl.ds(0, features)]
        first = iota((devices, slots), 1) == iota((devices, slots), 0) * capacity
        labels = dot(jnp.where(first, 1.0, 0.0).astype(BF16), received_ref[:, pl.ds(features, LANES)]).astype(BF16)
    labels_ref[...] = labels
    keyval_weight.product(rows, store_in(keyval))

    sender = floor_div(iota((devices, slots), 1), capacity) == iota((devices, slots), 0)
    filled = dot(lanes_of(labels, 0, per_device), jnp.where(sender, 1.0, 0.0).astype(BF16))
    lane = iota((1, slots), 1)
    place = (lane - floor_div(lane, capacity) * capacity).astype(F32)
    begin = jnp.zeros((1, slots), F32)
    for block in range(per_device):
        end = begin + filled[block : block + 1]
        bias[block : block + 1] = jnp.where((place >= begin) & (place < end), 0.0, MASKED)
        begin = end
    query_ref = query_rows()

    @pl.loop(0, features // LANES, unroll=unroll)
    def _(pair):
        columns = pl.ds(pl.multiple_of(pair * LANES, LANES), LANES)
        value_columns = pl.ds(pl.multiple_of(features + pair * LANES, LANES), LANES)
        keys, values = keyval[:, columns], keyval[:, value_columns]
        for block in range(per_device):
            block_rows = pl.ds(block * BLOCK, BLOCK)
            queries = split_heads(query_ref[block_rows, columns], head_size)
            scores = dot_t(queries, keys) + bias[block : block + 1]
            powers = jnp.exp(scores - jnp.max(scores, axis=-1, keepdims=True))
            output = share_out(powers, values)
            attended[block_rows, columns] = join_heads(output, head_size).astype(BF16)

    mesh_ref = mesh()

    def put_mid(columns, values):
        mid_ref[:, columns] = (mesh_ref[:, columns].astype(F32) + values).astype(BF16)

    out_weight.product(attended, put_mid)
    norm_ref[...] = normed(mid_ref[...], gain()[...]).astype(BF16)


def own_kernel(scale, norm_hbm, qkv_w, qkv_ref, norm_held, ready, qkv_held, arrived):
    features = norm_hbm.shape[1]
    norm = Fetch(norm_hbm, norm_held, ready.at[0])
    weight = Weight(qkv_w, qkv_held, arrived, 0, qkv_held.shape[0])
    weight.product(norm(), store_in(qkv_ref))
    queries = pl.ds(0, features)
    qkv_ref[:, queries] = (qkv_ref[:, queries].astype(F32) * scale).astype(BF16)


def hold_kernel(
    qkv_w, out_w, decode_w, qkv_hbm, after_hbm, kv_kept, out_kept, decode_kept, qkv_kept, ready, arrived
):
    tiles = out_kept.shape[0]
    weights = [
        Weight(qkv_w, kv_kept, arrived, 0, 2 * tiles, tiles),
        Weight(out_w, out_kept, arrived, 0, tiles, 0, 2 * tiles),
        Weight(decode_w, decode_kept, arrived, 0, 2 * tiles, 0, 3 * tiles),
    ]
    qkv = Fetch(qkv_hbm, qkv_kept, ready.at[0])
    for weight in weights:
        weight.wait()
    qkv()


def process_kernel(
    per_device, capacity, head_size, unroll, decode_unroll,
    me_ref, neighbour_ref, first_hbm, norm_hbm, second_hbm, qkv_ref, mid_hbm, gain_hbm, queries_ref, labels_hbm,
    kv_w, out_w, decode_w,
    answers_ref,
    mid_held, gain_held, labels_held, ready, picked,
    chosen, other, attended, mesh_out,
):
    features = mid_hbm.shape[1]
    odd = me_ref[0] % 2
    for block in range(per_device):
        rows = pl.ds(block * BLOCK, BLOCK)
        position = neighbour_ref[block] - me_ref[0] * per_device + per_device
        sides = ((first_hbm, 2 * (1 - odd)), (norm_hbm, 1), (second_hbm, 2 * odd))
        for source, side in sides:
            for place in range(per_device):
                @pl.when(position == side * per_device + place)
                def _():
                    block_rows = source.at[pl.ds(place * BLOCK, BLOCK)]
                    pltpu.make_async_copy(block_rows, chosen.at[rows], picked.at[block]).start()

    mid = Fetch(mid_hbm, mid_held, ready.at[0])
    gain = Fetch(gain_hbm, gain_held, ready.at[1])
    labels = Fetch(labels_hbm, labels_held, ready.at[2])
    for block in range(per_device):
        rows = pl.ds(block * BLOCK, BLOCK)
        pltpu.make_async_copy(norm_hbm.at[rows], chosen.at[rows], picked.at[block]).wait()
    product(chosen, kv_w, store_in(other))

    @pl.loop(0, features // LANES, unroll=unroll)
    def _(pair):
        columns = pl.ds(pl.multiple_of(pair * LANES, LANES), LANES)
        second = pl.ds(pl.multiple_of(features + pair * LANES, LANES), LANES)
        third = pl.ds(pl.multiple_of(2 * features + pair * LANES, LANES), LANES)
        for block in range(per_device):
            rows = pl.ds(block * BLOCK, BLOCK)
            queries = split_heads(qkv_ref[rows, columns], head_size)
            keys = jnp.concatenate([qkv_ref[rows, second], other[rows, columns]], axis=0)
            values = jnp.concatenate([qkv_ref[rows, third], other[rows, second]], axis=0)
            scores = dot_t(queries, keys)
            powers = jnp.exp(scores - jnp.max(scores, axis=-1, keepdims=True))
            sums = jnp.sum(powers, axis=-1, keepdims=True)
            output = dot(powers.astype(BF16), values) / sums
            attended[rows, columns] = join_heads(output, head_size).astype(BF16)

    mid_ref = mid()

    def put_out(columns, values):
        mesh_out[:, columns] = (mid_ref[:, columns].astype(F32) + values).astype(BF16)

    product(attended, out_w, put_out)
    chosen[...] = normed(mesh_out[...], gain()[...]).astype(BF16)
    product(chosen, decode_w, store_in(other))
    decode_points(
        per_device, capacity, head_size, decode_unroll, other, queries_ref, labels()[...], answers_ref
    )


def decode_points(per_device, capacity, head_size, unroll, other, queries_ref, labels, answers_ref):
    slots, features = answers_ref.shape
    devices = labels.shape[0]
    sender = floor_div(iota((slots, devices), 0), capacity) == iota((slots, devices), 1)
    filled = dot_t(jnp.where(sender, 1.0, 0.0).astype(BF16), lanes_of(labels, per_device, per_device))
    row = iota((slots, 1), 0)
    place = (row - floor_div(row, capacity) * capacity).astype(F32)
    reads, begin = [], jnp.zeros((slots, 1), F32)
    for block in range(per_device):
        end = begin + filled[:, block : block + 1]
        here = jnp.where((place >= begin) & (place < end), 1.0, 0.0)
        reads.append(jnp.broadcast_to(here, (slots, LANES)) > 0.5)
        begin = end

    @pl.loop(0, features // LANES, unroll=unroll)
    def _(pair):
        columns = pl.ds(pl.multiple_of(pair * LANES, LANES), LANES)
        second = pl.ds(pl.multiple_of(features + pair * LANES, LANES), LANES)
        queries = queries_ref[:, columns]
        even = even_lanes((slots, LANES), head_size)
        zero = jnp.zeros_like(queries)
        spread = jnp.concatenate([jnp.where(here, queries, zero) for here in reads], axis=1)
        keys, values = [
            jnp.concatenate(
                [split_heads(other[pl.ds(block * BLOCK, BLOCK), side], head_size) for block in range(per_device)], axis=1
            )
            for side in (columns, second)
        ]
        scores = dot_t(spread, keys)
        powers, sums = [], []
        for head in range(2):
            here = scores[:, head * BLOCK : (head + 1) * BLOCK]
            powers.append(jnp.exp(here - jnp.max(here, axis=-1, keepdims=True)))
            sums.append(jnp.sum(powers[head], axis=-1, keepdims=True))
        output = dot(jnp.concatenate(powers, axis=1).astype(BF16), values)
        answer = output[:, :LANES]
        for block in range(1, per_device):
            answer = jnp.where(reads[block], output[:, block * LANES : (block + 1) * LANES], answer)
        answers_ref[:, columns] = (answer / jnp.where(even, sums[0], sums[1])).astype(BF16)


def unpack_kernel(replies_ref, back_ref, out_w, update_hbm, decoded, update_ref, sent):
    features = out_w.shape[1]
    decoded[...] = dot(back_ref[...], replies_ref[...]).astype(BF16)
    copies = []
    for i in range(features // TILE):
        columns = pl.ds(i * TILE, TILE)
        update_ref[:, columns] = dot(decoded[...], out_w[:, columns]).astype(BF16)
        copies.append(pltpu.make_async_copy(update_ref.at[:, columns], update_hbm.at[:, columns], sent.at[i]))
        copies[-1].start()
    for copy in copies:
        copy.wait()


def call(kernel, operands, outs, scratch, name, flops, limit=VMEM_MIB, out_space=VMEM):
    return pl.pallas_call(
        kernel,
        out_shape=[jax.ShapeDtypeStruct(*out) if isinstance(out, tuple) else out for out in outs],
        in_specs=[pl.BlockSpec(memory_space=space) for space, _ in operands],
        out_specs=[pl.BlockSpec(memory_space=out_space) for _ in outs],
        scratch_shapes=scratch,
        name=name,
        cost_estimate=pl.CostEstimate(flops=flops, bytes_accessed=4 * MIB, transcendentals=0),
        compiler_params=pltpu.CompilerParams(vmem_limit_bytes=limit * MIB),
    )(*[pltpu.with_memory_space_constraint(value, HBM) if space is HBM else value for space, value in operands])


def held_like(*values):
    return [*[VMEM(value.shape, value.dtype) for value in values], pltpu.SemaphoreType.DMA((len(values),))]


def weights_held(count, features):
    return [VMEM((count, features, TILE), BF16), pltpu.SemaphoreType.DMA((count,))]


def on_device(
    grid_state,
    mesh_state,
    encode_block,
    neighbour_block,
    decode_block,
    encode_grid_gain,
    encode_mesh_gain,
    process_gain,
    decode_grid_gain,
    decode_mesh_gain,
    encode_query,
    encode_keyval,
    encode_out,
    process_qkv,
    process_out,
    decode_query,
    decode_keyval,
    decode_out,
):
    devices = lax.axis_size(AXES)
    me = lax.axis_index(AXES)
    grid_count, features = grid_state.shape
    mesh_rows = mesh_state.shape[0]
    per_device = mesh_rows // BLOCK
    total_blocks = per_device * devices
    capacity = max(4, 2 * grid_count // devices)
    slots = devices * capacity
    head_size = features // HEADS
    scale = head_size ** (-0.5)
    tiles = features // TILE
    me_row = me.astype(jnp.int32).reshape(1)
    encode_row, decode_row = encode_block.reshape(1, -1), decode_block.reshape(1, -1)
    encode_grid_gain, encode_mesh_gain, process_gain, decode_grid_gain, decode_mesh_gain = [
        gain.reshape(1, -1)
        for gain in (encode_grid_gain, encode_mesh_gain, process_gain, decode_grid_gain, decode_mesh_gain)
    ]

    def exchange(rows, *shape):
        return lax.all_to_all(rows.reshape(devices, *shape), AXES, split_axis=0, concat_axis=0, tiled=True)

    if by_tiles(capacity):
        payload = (capacity * features // LANES + 8, LANES)
        packed_shape = (devices, *payload)
    else:
        payload = (capacity, features + LANES)
        packed_shape = (slots, features + LANES)
    (packed,) = call(
        functools.partial(fill_kernel, devices, per_device, capacity),
        [(HBM, grid_state), (HBM, encode_row), (HBM, decode_row), (HBM, encode_grid_gain)],
        [(packed_shape, BF16)],
        [
            *held_like(grid_state, encode_row, decode_row, encode_grid_gain),
            VMEM(packed_shape, BF16),
            pltpu.SemaphoreType.DMA((PARTS,)),
        ],
        "fill",
        flops=600_000_000,
        out_space=ANY,
    )
    received = exchange(packed, *payload).reshape(packed_shape)
    query, packed_queries, back = call(
        functools.partial(query_kernel, devices, per_device, capacity, scale),
        [
            (HBM, mesh_state), (HBM, encode_mesh_gain), (HBM, encode_query),
            (HBM, grid_state), (HBM, decode_grid_gain), (HBM, decode_query), (HBM, decode_row),
        ],
        [((mesh_rows, features), BF16), ((slots, features), BF16), ((grid_count, slots), BF16)],
        [
            *held_like(mesh_state, encode_mesh_gain, grid_state, decode_grid_gain, decode_row),
            VMEM((grid_count, features), BF16),
            *weights_held(2 * tiles, features),
        ],
        "queries",
        flops=2_000_000_000,
    )
    arrived_queries = exchange(packed_queries, capacity, features).reshape(slots, features)
    mesh_mid, process_norm, labels = call(
        functools.partial(encode_kernel, per_device, capacity, head_size, ENCODE_UNROLL),
        [
            (ANY, received), (HBM, query), (HBM, mesh_state), (HBM, process_gain),
            (HBM, encode_keyval), (HBM, encode_out),
        ],
        [((mesh_rows, features), BF16), ((mesh_rows, features), BF16), ((devices, LANES), BF16)],
        [
            *held_like(received, query, mesh_state, process_gain),
            VMEM((slots, features), BF16),
            VMEM((slots, 2 * features), BF16),
            VMEM((mesh_rows, features), BF16),
            VMEM((8, slots), F32),
            *weights_held(3 * tiles, features),
        ],
        "encode",
        flops=5_000_000_000,
    )
    pairs = [(i, i ^ 1) for i in range(devices)]
    across = [(i, i + 1 if i % 2 else i - 1) for i in range(1, devices - 1)]
    first = lax.ppermute(process_norm, AXES, pairs)
    second = lax.ppermute(process_norm, AXES, across)
    (mesh_qkv,) = call(
        functools.partial(own_kernel, scale),
        [(HBM, process_norm), (HBM, process_qkv)],
        [((mesh_rows, 3 * features), BF16)],
        [
            *held_like(process_norm),
            VMEM((3 * tiles, features, TILE), BF16),
            pltpu.SemaphoreType.DMA((3 * tiles,)),
        ],
        "own",
        flops=2_000_000_000,
    )
    kv_w, out_w, decode_w, mesh_qkv = call(
        hold_kernel,
        [(HBM, process_qkv), (HBM, process_out), (HBM, decode_keyval), (HBM, mesh_qkv), (ANY, arrived_queries)],
        [
            *[VMEM((count * tiles, features, TILE), BF16) for count in (2, 1, 2)],
            VMEM(mesh_qkv.shape, BF16),
        ],
        [pltpu.SemaphoreType.DMA((1,)), pltpu.SemaphoreType.DMA((5 * tiles,))],
        "hold",
        flops=2_000_000_000,
        limit=36,
    )
    (answers,) = call(
        functools.partial(process_kernel, per_device, capacity, head_size, PROCESS_UNROLL, DECODE_UNROLL),
        [
            (SMEM, me_row), (SMEM, neighbour_block), (ANY, first), (ANY, process_norm), (ANY, second),
            (VMEM, mesh_qkv), (HBM, mesh_mid), (HBM, decode_mesh_gain), (VMEM, arrived_queries), (HBM, labels),
            (VMEM, kv_w), (VMEM, out_w), (VMEM, decode_w),
        ],
        [((slots, features), BF16)],
        [
            *held_like(mesh_mid, decode_mesh_gain, labels),
            pltpu.SemaphoreType.DMA((per_device,)),
            VMEM((mesh_rows, features), BF16),
            VMEM((mesh_rows, 2 * features), BF16),
            VMEM((mesh_rows, features), BF16),
            VMEM((mesh_rows, features), BF16),
        ],
        "process",
        flops=8_000_000_000,
        limit=36,
    )
    replies = exchange(answers, capacity, features).reshape(slots, features)
    (update,) = call(
        unpack_kernel,
        [(VMEM, replies), (VMEM, back), (VMEM, decode_out)],
        [((grid_count, features), BF16)],
        [
            VMEM((grid_count, features), BF16),
            VMEM((grid_count, features), BF16),
            pltpu.SemaphoreType.DMA((tiles,)),
        ],
        "unpack",
        flops=1_000_000_000,
        limit=24,
        out_space=ANY,
    )
    return update


def solution(mesh):
    in_specs = (P(AXES, None), P(AXES, None), P(AXES), P(AXES), P(AXES), *[P()] * 13)
    return jax.shard_map(
        on_device, mesh=mesh, in_specs=in_specs, out_specs=P(AXES, None), check_vma=False
    )
```

```python
import functools

import jax
import jax.numpy as jnp
from jax import lax
from jax.experimental import pallas as pl
from jax.experimental.pallas import tpu as pltpu
from jax.sharding import PartitionSpec as P

HEADS = 16
BLOCK = 128
TILE = 512
LANES = 128
MASKED = -1e30
VMEM_MIB = 56
PARTS = 4
ENCODE_UNROLL = 8
PROCESS_UNROLL = 8
DECODE_UNROLL = 8
ANY, HBM, VMEM, SMEM = pl.ANY, pltpu.HBM, pltpu.VMEM, pltpu.SMEM
AXES = ("gx", "gy")
F32 = jnp.float32
BF16 = jnp.bfloat16
MIB = 1024 * 1024


def iota(shape, dim):
    return lax.broadcasted_iota(jnp.int32, shape, dim)


def floor_div(values, by):
    return jnp.floor((values.astype(F32) + 0.5) * (1.0 / by)).astype(jnp.int32)


def dot(left, right):
    return jnp.dot(left, right, preferred_element_type=F32)


def dot_t(left, right):
    return lax.dot_general(left, right, (((1,), (1,)), ((), ())), preferred_element_type=F32)


def dot_tl(left, right):
    return lax.dot_general(left, right, (((0,), (0,)), ((), ())), preferred_element_type=F32)


def normed(values, gain):
    wide = values.astype(F32)
    return wide * lax.rsqrt(jnp.mean(wide * wide, axis=-1, keepdims=True) + 1e-06) * gain


def block_hits(blocks, total_blocks):
    hits = iota((total_blocks, blocks.shape[1]), 0) == blocks
    return jnp.where(hits, 1.0, 0.0).astype(F32)


def block_counts(hits):
    counts = jnp.sum(hits, axis=1, keepdims=True)
    return jnp.broadcast_to(counts, (hits.shape[0], LANES)).astype(BF16)


def slots_of(hits, per_device, capacity):
    total_blocks, points = hits.shape
    earlier = jnp.where(iota((points, points), 0) < iota((points, points), 1), 1.0, 0.0)
    before = dot(hits.astype(BF16), earlier.astype(BF16))
    row, column = iota((total_blocks, total_blocks), 0), iota((total_blocks, total_blocks), 1)
    mates = (floor_div(row, per_device) == floor_div(column, per_device)) & (column < row)
    offset = dot(jnp.where(mates, 1.0, 0.0).astype(BF16), block_counts(hits))[:, :1]
    owner = floor_div(iota((total_blocks, 1), 0), per_device)
    base = owner.astype(F32) * capacity + offset
    return jnp.sum(hits * (base + before), axis=0, keepdims=True).astype(jnp.int32)


def placement(slot, slots):
    return jnp.where(iota((slots, slot.shape[1]), 0) == slot, 1.0, 0.0).astype(BF16)


class Fetch:
    def __init__(self, source, held, ready):
        self.copy = pltpu.make_async_copy(source, held, ready)
        self.held = held
        self.waiting = True
        self.copy.start()

    def __call__(self):
        if self.waiting:
            self.copy.wait()
            self.waiting = False
        return self.held


class Weight:
    def __init__(self, source, held, ready, base, count, first=0, semaphore=None):
        semaphore = base if semaphore is None else semaphore
        self.source, self.held, self.ready, self.base, self.count = source, held, ready, base, count
        self.semaphore = semaphore

        @pl.loop(0, count)
        def _(i):
            columns = pl.ds(pl.multiple_of((first + i) * TILE, TILE), TILE)
            pltpu.make_async_copy(source.at[:, columns], held.at[base + i], ready.at[semaphore + i]).start()

    def arrive(self, i):
        held = self.held.at[self.base + i]
        pltpu.make_async_copy(self.source.at[:, pl.ds(0, TILE)], held, self.ready.at[self.semaphore + i]).wait()
        return held

    def wait(self):
        @pl.loop(0, self.count)
        def _(i):
            self.arrive(i)

    def product(self, rows, put):
        for i in range(self.count):
            put(pl.ds(i * TILE, TILE), dot(rows[...], self.arrive(i)[...]))


def product(rows, held, put):
    for i in range(held.shape[0]):
        put(pl.ds(i * TILE, TILE), dot(rows[...], held[i]))


def store_in(ref):
    def put(columns, values):
        ref[:, columns] = values.astype(ref.dtype)

    return put


def count_lanes(encode_counts, decode_counts, devices, per_device):
    total_blocks = encode_counts.shape[0]
    lane = iota((devices, LANES), 1)
    labels = jnp.zeros((devices, LANES), F32)
    for kind, counts in enumerate((encode_counts, decode_counts)):
        for block in range(per_device):
            wanted = iota((devices, total_blocks), 0) * per_device + block
            wanted = jnp.where(iota((devices, total_blocks), 1) == wanted, 1.0, 0.0).astype(BF16)
            labels = labels + jnp.where(lane == kind * per_device + block, dot(wanted, counts), 0.0)
    return labels.astype(BF16)


def by_tiles(capacity):
    return capacity % 16 == 0


def fill_kernel(
    devices, per_device, capacity,
    state_hbm, encode_hbm, decode_hbm, gain_hbm, packed_hbm,
    state_held, encode_held, decode_held, gain_held, ready, packed_ref, sent,
):
    encode = Fetch(encode_hbm, encode_held, ready.at[0])
    decode = Fetch(decode_hbm, decode_held, ready.at[1])
    state = Fetch(state_hbm, state_held, ready.at[2])
    gain = Fetch(gain_hbm, gain_held, ready.at[3])
    total_blocks, slots = devices * per_device, devices * capacity
    encode_hits = block_hits(encode()[...], total_blocks)
    place = placement(slots_of(encode_hits, per_device, capacity), slots)
    decode_hits = block_hits(decode()[...], total_blocks)
    labels = count_lanes(block_counts(encode_hits), block_counts(decode_hits), devices, per_device)
    norm = normed(state()[...], gain()[...]).astype(BF16)
    features = norm.shape[1]
    copies = []

    def send(place):
        copies.append(pltpu.make_async_copy(packed_ref.at[place], packed_hbm.at[place], sent.at[len(copies)]))
        copies[-1].start()

    if by_tiles(capacity):
        last = pl.ds(features // LANES * capacity, 8)
        packed_ref[:, last] = jnp.broadcast_to(labels[:, None, :], (devices, 8, LANES))
        part = devices // PARTS
        for i in range(PARTS):
            owners = pl.ds(i * part, part)
            rows = dot(place[i * part * capacity : (i + 1) * part * capacity], norm).astype(BF16)
            for tile in range(features // LANES):
                columns = rows[:, tile * LANES : (tile + 1) * LANES].reshape(part, capacity, LANES)
                packed_ref[owners, pl.ds(tile * capacity, capacity)] = columns
            send(owners)
    else:
        packed_ref[:, pl.ds(0, features)] = dot(place, norm).astype(BF16)
        owner = floor_div(iota((slots, devices), 0), capacity) == iota((slots, devices), 1)
        packed_ref[:, pl.ds(features, LANES)] = dot(jnp.where(owner, 1.0, 0.0).astype(BF16), labels).astype(BF16)
        send(slice(None))
    for copy in copies:
        copy.wait()


def query_kernel(
    devices, per_device, capacity, scale,
    mesh_hbm, mesh_gain_hbm, encode_w, grid_hbm, grid_gain_hbm, decode_w, decode_hbm,
    query_ref, packed_ref, back_ref,
    mesh_held, mesh_gain_held, grid_held, grid_gain_held, decode_held, ready,
    norm_ref, weights, arrived,
):
    decode = Fetch(decode_hbm, decode_held, ready.at[0])
    grid = Fetch(grid_hbm, grid_held, ready.at[1])
    grid_gain = Fetch(grid_gain_hbm, grid_gain_held, ready.at[2])
    mesh = Fetch(mesh_hbm, mesh_held, ready.at[3])
    mesh_gain = Fetch(mesh_gain_hbm, mesh_gain_held, ready.at[4])
    count = encode_w.shape[1] // TILE
    decode_weight = Weight(decode_w, weights, arrived, 0, count)
    encode_weight = Weight(encode_w, weights, arrived, count, count)
    slots = packed_ref.shape[0]
    hits = block_hits(decode()[...], devices * per_device)
    place = placement(slots_of(hits, per_device, capacity), slots)
    back_ref[...] = place.T
    norm_ref[...] = normed(grid()[...], grid_gain()[...]).astype(BF16)

    def put_packed(columns, values):
        rounded = (values.astype(BF16).astype(F32) * scale).astype(BF16)
        packed_ref[:, columns] = dot(place, rounded).astype(BF16)

    decode_weight.product(norm_ref, put_packed)
    norm_ref[...] = normed(mesh()[...], mesh_gain()[...]).astype(BF16)

    def put_query(columns, values):
        query_ref[:, columns] = (values.astype(BF16).astype(F32) * scale).astype(BF16)

    encode_weight.product(norm_ref, put_query)


def lanes_of(labels, first, count):
    row, lane = iota((8, LANES), 0), iota((8, LANES), 1)
    wanted = (lane == row + first) & (row < count)
    return dot_t(jnp.where(wanted, 1.0, 0.0).astype(BF16), labels).astype(BF16)


def even_lanes(shape, head_size):
    return iota(shape, len(shape) - 1) < head_size


def split_heads(values, head_size):
    even = even_lanes(values.shape, head_size)
    zero = jnp.zeros_like(values)
    return jnp.concatenate([jnp.where(even, values, zero), jnp.where(even, zero, values)], axis=0)


def join_heads(values, head_size):
    rows = values.shape[0] // 2
    even = even_lanes((rows, values.shape[1]), head_size)
    return jnp.where(even, values[:rows], values[rows:])


def share_out(powers, values):
    output = dot(powers.astype(BF16), jnp.concatenate([values, jnp.ones_like(values)], axis=1))
    return output[:, :LANES] / output[:, LANES:]


def keys_first(scores):
    powers = jnp.exp(scores - jnp.max(scores, axis=0, keepdims=True))
    return powers.astype(BF16), 1.0 / jnp.sum(powers, axis=0, keepdims=True)


def encode_kernel(
    per_device, capacity, head_size, unroll,
    received_hbm, query_hbm, mesh_hbm, gain_hbm, keyval_w, out_w,
    mid_ref, norm_ref, labels_ref,
    received_held, query_held, mesh_held, gain_held, ready,
    rows_ref, keyval, attended, bias, weights, arrived,
):
    features = mid_ref.shape[1]
    devices = labels_ref.shape[0]
    slots = devices * capacity
    kv_count, out_count = keyval_w.shape[1] // TILE, features // TILE
    received = Fetch(received_hbm, received_held, ready.at[0])
    keyval_weight = Weight(keyval_w, weights, arrived, 0, kv_count)
    query_rows = Fetch(query_hbm, query_held, ready.at[1])
    out_weight = Weight(out_w, weights, arrived, kv_count, out_count)
    mesh = Fetch(mesh_hbm, mesh_held, ready.at[2])
    gain = Fetch(gain_hbm, gain_held, ready.at[3])
    received_ref = received()
    if by_tiles(capacity):
        for tile in range(features // LANES):
            part = received_ref[:, pl.ds(tile * capacity, capacity), :]
            rows_ref[:, pl.ds(tile * LANES, LANES)] = part.reshape(slots, LANES)
        last = received_ref[:, pl.ds(features // LANES * capacity, 8), :]
        labels = jnp.max(last.astype(F32), axis=1).astype(BF16)
        rows = rows_ref
    else:
        rows = received_ref.at[:, pl.ds(0, features)]
        first = iota((devices, slots), 1) == iota((devices, slots), 0) * capacity
        labels = dot(jnp.where(first, 1.0, 0.0).astype(BF16), received_ref[:, pl.ds(features, LANES)]).astype(BF16)
    labels_ref[...] = labels
    keyval_weight.product(rows, store_in(keyval))

    sender = floor_div(iota((devices, slots), 1), capacity) == iota((devices, slots), 0)
    filled = dot(lanes_of(labels, 0, per_device), jnp.where(sender, 1.0, 0.0).astype(BF16))
    lane = iota((1, slots), 1)
    place = (lane - floor_div(lane, capacity) * capacity).astype(F32)
    begin = jnp.zeros((1, slots), F32)
    for block in range(per_device):
        end = begin + filled[block : block + 1]
        bias[block : block + 1] = jnp.where((place >= begin) & (place < end), 0.0, MASKED)
        begin = end
    query_ref = query_rows()

    @pl.loop(0, features // LANES, unroll=unroll)
    def _(pair):
        columns = pl.ds(pl.multiple_of(pair * LANES, LANES), LANES)
        value_columns = pl.ds(pl.multiple_of(features + pair * LANES, LANES), LANES)
        keys, values = keyval[:, columns], keyval[:, value_columns]
        for block in range(per_device):
            block_rows = pl.ds(block * BLOCK, BLOCK)
            queries = split_heads(query_ref[block_rows, columns], head_size)
            scores = dot_t(queries, keys) + bias[block : block + 1]
            powers = jnp.exp(scores - jnp.max(scores, axis=-1, keepdims=True))
            output = share_out(powers, values)
            attended[block_rows, columns] = join_heads(output, head_size).astype(BF16)

    mesh_ref = mesh()

    def put_mid(columns, values):
        mid_ref[:, columns] = (mesh_ref[:, columns].astype(F32) + values).astype(BF16)

    out_weight.product(attended, put_mid)
    norm_ref[...] = normed(mid_ref[...], gain()[...]).astype(BF16)


def own_kernel(scale, norm_hbm, qkv_w, qkv_ref, norm_held, ready, qkv_held, arrived):
    features = norm_hbm.shape[1]
    norm = Fetch(norm_hbm, norm_held, ready.at[0])
    weight = Weight(qkv_w, qkv_held, arrived, 0, qkv_held.shape[0])
    weight.product(norm(), store_in(qkv_ref))
    queries = pl.ds(0, features)
    qkv_ref[:, queries] = (qkv_ref[:, queries].astype(F32) * scale).astype(BF16)


def hold_kernel(
    qkv_w, out_w, qkv_hbm, after_hbm, kv_kept, out_kept, qkv_kept, ready, arrived
):
    tiles = out_kept.shape[0]
    weights = [
        Weight(qkv_w, kv_kept, arrived, 0, 2 * tiles, tiles),
        Weight(out_w, out_kept, arrived, 0, tiles, 0, 2 * tiles),
    ]
    qkv = Fetch(qkv_hbm, qkv_kept, ready.at[0])
    for weight in weights:
        weight.wait()
    qkv()


def process_kernel(
    per_device, capacity, head_size, unroll, decode_unroll,
    me_ref, neighbour_ref, first_hbm, norm_hbm, second_hbm, qkv_ref, mid_hbm, gain_hbm, queries_ref, labels_hbm,
    kv_w, out_w, decode_w,
    answers_ref,
    mid_held, gain_held, labels_held, ready, picked,
    chosen, other, attended, mesh_out, decode_held, arrived,
):
    features = mid_hbm.shape[1]
    odd = me_ref[0] % 2
    for block in range(per_device):
        rows = pl.ds(block * BLOCK, BLOCK)
        position = neighbour_ref[block] - me_ref[0] * per_device + per_device
        sides = ((first_hbm, 2 * (1 - odd)), (norm_hbm, 1), (second_hbm, 2 * odd))
        for source, side in sides:
            for place in range(per_device):
                @pl.when(position == side * per_device + place)
                def _():
                    block_rows = source.at[pl.ds(place * BLOCK, BLOCK)]
                    pltpu.make_async_copy(block_rows, chosen.at[rows], picked.at[block]).start()

    mid = Fetch(mid_hbm, mid_held, ready.at[0])
    gain = Fetch(gain_hbm, gain_held, ready.at[1])
    labels = Fetch(labels_hbm, labels_held, ready.at[2])
    decode_weight = Weight(decode_w, decode_held, arrived, 0, decode_held.shape[0])
    for block in range(per_device):
        rows = pl.ds(block * BLOCK, BLOCK)
        pltpu.make_async_copy(norm_hbm.at[rows], chosen.at[rows], picked.at[block]).wait()
    product(chosen, kv_w, store_in(other))

    @pl.loop(0, features // LANES, unroll=unroll)
    def _(pair):
        columns = pl.ds(pl.multiple_of(pair * LANES, LANES), LANES)
        second = pl.ds(pl.multiple_of(features + pair * LANES, LANES), LANES)
        third = pl.ds(pl.multiple_of(2 * features + pair * LANES, LANES), LANES)
        for block in range(per_device):
            rows = pl.ds(block * BLOCK, BLOCK)
            queries = split_heads(qkv_ref[rows, columns], head_size)
            keys = jnp.concatenate([qkv_ref[rows, second], other[rows, columns]], axis=0)
            values = jnp.concatenate([qkv_ref[rows, third], other[rows, second]], axis=0)
            scores = dot_t(queries, keys)
            powers = jnp.exp(scores - jnp.max(scores, axis=-1, keepdims=True))
            sums = jnp.sum(powers, axis=-1, keepdims=True)
            output = dot(powers.astype(BF16), values) / sums
            attended[rows, columns] = join_heads(output, head_size).astype(BF16)

    mid_ref = mid()

    def put_out(columns, values):
        mesh_out[:, columns] = (mid_ref[:, columns].astype(F32) + values).astype(BF16)

    product(attended, out_w, put_out)
    chosen[...] = normed(mesh_out[...], gain()[...]).astype(BF16)
    decode_weight.wait()
    product(chosen, decode_held, store_in(other))
    decode_points(
        per_device, capacity, head_size, decode_unroll, other, queries_ref, labels()[...], answers_ref
    )


def decode_points(per_device, capacity, head_size, unroll, other, queries_ref, labels, answers_ref):
    slots, features = answers_ref.shape
    devices = labels.shape[0]
    sender = floor_div(iota((slots, devices), 0), capacity) == iota((slots, devices), 1)
    filled = dot_t(jnp.where(sender, 1.0, 0.0).astype(BF16), lanes_of(labels, per_device, per_device))
    row = iota((slots, 1), 0)
    place = (row - floor_div(row, capacity) * capacity).astype(F32)
    reads, begin = [], jnp.zeros((slots, 1), F32)
    for block in range(per_device):
        end = begin + filled[:, block : block + 1]
        here = jnp.where((place >= begin) & (place < end), 1.0, 0.0)
        reads.append(jnp.broadcast_to(here, (slots, LANES)) > 0.5)
        begin = end

    @pl.loop(0, features // LANES, unroll=unroll)
    def _(pair):
        columns = pl.ds(pl.multiple_of(pair * LANES, LANES), LANES)
        second = pl.ds(pl.multiple_of(features + pair * LANES, LANES), LANES)
        queries = queries_ref[:, columns]
        even = even_lanes((slots, LANES), head_size)
        zero = jnp.zeros_like(queries)
        spread = jnp.concatenate([jnp.where(here, queries, zero) for here in reads], axis=1)
        keys, values = [
            jnp.concatenate(
                [split_heads(other[pl.ds(block * BLOCK, BLOCK), side], head_size) for block in range(per_device)], axis=1
            )
            for side in (columns, second)
        ]
        scores = dot_t(spread, keys)
        powers, sums = [], []
        for head in range(2):
            here = scores[:, head * BLOCK : (head + 1) * BLOCK]
            powers.append(jnp.exp(here - jnp.max(here, axis=-1, keepdims=True)))
            sums.append(jnp.sum(powers[head], axis=-1, keepdims=True))
        output = dot(jnp.concatenate(powers, axis=1).astype(BF16), values)
        answer = output[:, :LANES]
        for block in range(1, per_device):
            answer = jnp.where(reads[block], output[:, block * LANES : (block + 1) * LANES], answer)
        answers_ref[:, columns] = (answer / jnp.where(even, sums[0], sums[1])).astype(BF16)


def unpack_kernel(replies_ref, back_ref, out_w, update_hbm, decoded, update_ref, sent):
    features = out_w.shape[1]
    decoded[...] = dot(back_ref[...], replies_ref[...]).astype(BF16)
    copies = []
    for i in range(features // TILE):
        columns = pl.ds(i * TILE, TILE)
        update_ref[:, columns] = dot(decoded[...], out_w[:, columns]).astype(BF16)
        copies.append(pltpu.make_async_copy(update_ref.at[:, columns], update_hbm.at[:, columns], sent.at[i]))
        copies[-1].start()
    for copy in copies:
        copy.wait()


def call(kernel, operands, outs, scratch, name, flops, limit=VMEM_MIB, out_space=VMEM):
    return pl.pallas_call(
        kernel,
        out_shape=[jax.ShapeDtypeStruct(*out) if isinstance(out, tuple) else out for out in outs],
        in_specs=[pl.BlockSpec(memory_space=space) for space, _ in operands],
        out_specs=[pl.BlockSpec(memory_space=out_space) for _ in outs],
        scratch_shapes=scratch,
        name=name,
        cost_estimate=pl.CostEstimate(flops=flops, bytes_accessed=4 * MIB, transcendentals=0),
        compiler_params=pltpu.CompilerParams(vmem_limit_bytes=limit * MIB),
    )(*[pltpu.with_memory_space_constraint(value, HBM) if space is HBM else value for space, value in operands])


def held_like(*values):
    return [*[VMEM(value.shape, value.dtype) for value in values], pltpu.SemaphoreType.DMA((len(values),))]


def weights_held(count, features):
    return [VMEM((count, features, TILE), BF16), pltpu.SemaphoreType.DMA((count,))]


def on_device(
    grid_state,
    mesh_state,
    encode_block,
    neighbour_block,
    decode_block,
    encode_grid_gain,
    encode_mesh_gain,
    process_gain,
    decode_grid_gain,
    decode_mesh_gain,
    encode_query,
    encode_keyval,
    encode_out,
    process_qkv,
    process_out,
    decode_query,
    decode_keyval,
    decode_out,
):
    devices = lax.axis_size(AXES)
    me = lax.axis_index(AXES)
    grid_count, features = grid_state.shape
    mesh_rows = mesh_state.shape[0]
    per_device = mesh_rows // BLOCK
    total_blocks = per_device * devices
    capacity = max(4, 2 * grid_count // devices)
    slots = devices * capacity
    head_size = features // HEADS
    scale = head_size ** (-0.5)
    tiles = features // TILE
    me_row = me.astype(jnp.int32).reshape(1)
    encode_row, decode_row = encode_block.reshape(1, -1), decode_block.reshape(1, -1)
    encode_grid_gain, encode_mesh_gain, process_gain, decode_grid_gain, decode_mesh_gain = [
        gain.reshape(1, -1)
        for gain in (encode_grid_gain, encode_mesh_gain, process_gain, decode_grid_gain, decode_mesh_gain)
    ]

    def exchange(rows, *shape):
        return lax.all_to_all(rows.reshape(devices, *shape), AXES, split_axis=0, concat_axis=0, tiled=True)

    if by_tiles(capacity):
        payload = (capacity * features // LANES + 8, LANES)
        packed_shape = (devices, *payload)
    else:
        payload = (capacity, features + LANES)
        packed_shape = (slots, features + LANES)
    (packed,) = call(
        functools.partial(fill_kernel, devices, per_device, capacity),
        [(HBM, grid_state), (HBM, encode_row), (HBM, decode_row), (HBM, encode_grid_gain)],
        [(packed_shape, BF16)],
        [
            *held_like(grid_state, encode_row, decode_row, encode_grid_gain),
            VMEM(packed_shape, BF16),
            pltpu.SemaphoreType.DMA((PARTS,)),
        ],
        "fill",
        flops=600_000_000,
        out_space=ANY,
    )
    received = exchange(packed, *payload).reshape(packed_shape)
    query, packed_queries, back = call(
        functools.partial(query_kernel, devices, per_device, capacity, scale),
        [
            (HBM, mesh_state), (HBM, encode_mesh_gain), (HBM, encode_query),
            (HBM, grid_state), (HBM, decode_grid_gain), (HBM, decode_query), (HBM, decode_row),
        ],
        [((mesh_rows, features), BF16), ((slots, features), BF16), ((grid_count, slots), BF16)],
        [
            *held_like(mesh_state, encode_mesh_gain, grid_state, decode_grid_gain, decode_row),
            VMEM((grid_count, features), BF16),
            *weights_held(2 * tiles, features),
        ],
        "queries",
        flops=2_000_000_000,
    )
    arrived_queries = exchange(packed_queries, capacity, features).reshape(slots, features)
    mesh_mid, process_norm, labels = call(
        functools.partial(encode_kernel, per_device, capacity, head_size, ENCODE_UNROLL),
        [
            (ANY, received), (HBM, query), (HBM, mesh_state), (HBM, process_gain),
            (HBM, encode_keyval), (HBM, encode_out),
        ],
        [((mesh_rows, features), BF16), ((mesh_rows, features), BF16), ((devices, LANES), BF16)],
        [
            *held_like(received, query, mesh_state, process_gain),
            VMEM((slots, features), BF16),
            VMEM((slots, 2 * features), BF16),
            VMEM((mesh_rows, features), BF16),
            VMEM((8, slots), F32),
            *weights_held(3 * tiles, features),
        ],
        "encode",
        flops=5_000_000_000,
    )
    pairs = [(i, i ^ 1) for i in range(devices)]
    across = [(i, i + 1 if i % 2 else i - 1) for i in range(1, devices - 1)]
    first = lax.ppermute(process_norm, AXES, pairs)
    second = lax.ppermute(process_norm, AXES, across)
    (mesh_qkv,) = call(
        functools.partial(own_kernel, scale),
        [(HBM, process_norm), (HBM, process_qkv)],
        [((mesh_rows, 3 * features), BF16)],
        [
            *held_like(process_norm),
            VMEM((3 * tiles, features, TILE), BF16),
            pltpu.SemaphoreType.DMA((3 * tiles,)),
        ],
        "own",
        flops=2_000_000_000,
    )
    kv_w, out_w, mesh_qkv = call(
        hold_kernel,
        [(HBM, process_qkv), (HBM, process_out), (HBM, mesh_qkv), (ANY, arrived_queries)],
        [
            *[VMEM((count * tiles, features, TILE), BF16) for count in (2, 1)],
            VMEM(mesh_qkv.shape, BF16),
        ],
        [pltpu.SemaphoreType.DMA((1,)), pltpu.SemaphoreType.DMA((3 * tiles,))],
        "hold",
        flops=2_000_000_000,
        limit=36,
    )
    (answers,) = call(
        functools.partial(process_kernel, per_device, capacity, head_size, PROCESS_UNROLL, DECODE_UNROLL),
        [
            (SMEM, me_row), (SMEM, neighbour_block), (ANY, first), (ANY, process_norm), (ANY, second),
            (VMEM, mesh_qkv), (HBM, mesh_mid), (HBM, decode_mesh_gain), (VMEM, arrived_queries), (HBM, labels),
            (VMEM, kv_w), (VMEM, out_w), (HBM, decode_keyval),
        ],
        [((slots, features), BF16)],
        [
            *held_like(mesh_mid, decode_mesh_gain, labels),
            pltpu.SemaphoreType.DMA((per_device,)),
            VMEM((mesh_rows, features), BF16),
            VMEM((mesh_rows, 2 * features), BF16),
            VMEM((mesh_rows, features), BF16),
            VMEM((mesh_rows, features), BF16),
            *weights_held(2 * tiles, features),
        ],
        "process",
        flops=8_000_000_000,
        limit=36,
    )
    replies = exchange(answers, capacity, features).reshape(slots, features)
    (update,) = call(
        unpack_kernel,
        [(VMEM, replies), (VMEM, back), (VMEM, decode_out)],
        [((grid_count, features), BF16)],
        [
            VMEM((grid_count, features), BF16),
            VMEM((grid_count, features), BF16),
            pltpu.SemaphoreType.DMA((tiles,)),
        ],
        "unpack",
        flops=1_000_000_000,
        limit=24,
        out_space=ANY,
    )
    return update


def solution(mesh):
    in_specs = (P(AXES, None), P(AXES, None), P(AXES), P(AXES), P(AXES), *[P()] * 13)
    return jax.shard_map(
        on_device, mesh=mesh, in_specs=in_specs, out_specs=P(AXES, None), check_vma=False
    )
```
